128 devices in a mesh: hi: 16 (over y, x), lo: 8 (over z, core).
Axes of the slice: x: 4, y: 4, z: 4, core: 2. Of those that a mesh axis runs over, the one named last changes fastest.
Arguments:
- previous: float32 [32, 2097152], P(None, ('hi', 'lo')), may hold values from -6 to 6
- current: float32 [32, 2097152], P(None, ('hi', 'lo')), may hold values from -6 to 6
- field_levels: int32 [21], replicated, may hold values from -4 to 4
- bond_levels: int32 [20], replicated, may hold values from 1 to 3
Outputs:
- ortho_block: float32 [32, 2097152], P(None, ('hi', 'lo'))
- upper_factor: float32 [32, 32], replicated
The draws below stay inside these ranges and needn't reach their ends.
All inputs are finite; a program needn't handle non-finite values.
Results may differ from the reference program's by a relative error of at most 0.00005.
Values sent between devices are 32-bit elements; how exact they have to be, the bound alone decides.
A program may use at most 64 MiB of HBM per device.

```python
import jax
import jax.numpy as jnp
from jax import lax

NVEC = 32
LB = 14
GB = 7
SITES = 21
BONDS = 20
DIM = 2097152


def place_ends(array, stream_key, low, largest):
    longest = array.shape.index(max(array.shape))
    spots = []
    for shift in (0, 1):
        where = [jax.random.randint(jax.random.fold_in(stream_key, axis), (), 0, length) for axis, length in enumerate(array.shape)]
        where[longest] = (where[longest] + shift) % array.shape[longest]
        spots.append(tuple(where))
    return array.at[spots[0]].set(low).at[spots[1]].set(largest)


def block_scale(key, dims, pieces, low, high):
    def one(dim, blocks):
        draws = jax.random.uniform(jax.random.fold_in(jax.random.fold_in(key, 6), dim), (blocks,), jnp.float32, low / len(pieces), high / len(pieces))
        return jnp.repeat(jnp.exp(draws), dims[dim] // blocks).reshape((-1,) + (1,) * (len(dims) - dim - 1))

    level = one(*pieces[0])
    for cut in pieces[1:]:
        level = level * one(*cut)
    return level


def scatter_about(rng, extent, scale, most, shards=(), kind=jnp.bfloat16):
    array = jax.random.normal(rng, extent, jnp.float32) * scale
    if len(shards) > 0:
        array = block_scale(rng, extent, shards, -0.22, 0.18) * array
    return jnp.clip(array, min=-most, max=most).astype(kind)


def setup_inputs(seed: int = 0) -> dict:
    arg_keys = jax.random.split(jax.random.key(seed), 5)
    previous = scatter_about(arg_keys[0], (NVEC, DIM), 1.0, 6.0, ((1, 128),), jnp.float32)
    current = scatter_about(arg_keys[1], (NVEC, DIM), 1.0, 6.0, ((1, 128),), jnp.float32)
    field_levels = place_ends(jax.random.randint(arg_keys[2], (SITES,), -4, 5), jax.random.fold_in(arg_keys[2], 1), -4, 4).astype(jnp.int32)
    bond_levels = place_ends(jax.random.randint(arg_keys[3], (BONDS,), 1, 4), jax.random.fold_in(arg_keys[3], 1), 1, 3).astype(jnp.int32)
    return {"previous": previous, "current": current, "field_levels": field_levels, "bond_levels": bond_levels}


FIELD_STEP = 0.75
COUPLING_STEP = 0.5

def site_bit(site_number):
    if site_number < GB:
        return LB - GB + site_number
    if site_number < LB:
        return site_number - GB
    return site_number

def pair_flip(values, first_bit, second_bit, bit_count):
    top_bit = max(first_bit, second_bit)
    low_bit = min(first_bit, second_bit)
    vectors = values.shape[0]
    shaped = values.reshape(vectors, 2 ** (bit_count - top_bit - 1), 2, 2 ** (top_bit - low_bit - 1), 2, 2 ** low_bit)
    flipped = jnp.flip(shaped, axis=(2, 4))
    opposite = (1.0 - jnp.eye(2, dtype=jnp.float32)).reshape(1, 1, 2, 1, 2, 1)
    return (flipped * opposite).reshape(values.shape)

def reference(previous, current, field_levels, bond_levels):
    full_index = lax.iota(jnp.int32, DIM)
    spin_values = [0.5 - (full_index >> site_bit(site_number) & 1).astype(jnp.float32) for site_number in range(SITES)]
    fields = FIELD_STEP * field_levels.astype(jnp.float32)
    couplings = COUPLING_STEP * bond_levels.astype(jnp.float32)
    diagonal = jnp.zeros((DIM,), jnp.float32)
    for site_number in range(SITES):
        diagonal = diagonal + fields[site_number] * spin_values[site_number]
        if site_number < SITES - 1:
            diagonal = diagonal + couplings[site_number] * spin_values[site_number] * spin_values[site_number + 1]
    applied = diagonal[None, :] * current
    for site_number in range(SITES - 1):
        applied = applied + 0.5 * couplings[site_number] * pair_flip(current, site_bit(site_number), site_bit(site_number + 1), SITES)
    filtered = 4.0 / SITES * applied - previous
    gram_matrix = jnp.dot(filtered, filtered.T, precision=lax.Precision.HIGHEST) / DIM
    lower_factor = jnp.linalg.cholesky(gram_matrix)
    inverse = jax.scipy.linalg.solve_triangular(lower_factor, jnp.eye(NVEC, dtype=jnp.float32), lower=True)
    ortho_block = jnp.dot(inverse, filtered, precision=lax.Precision.HIGHEST)
    return (ortho_block, lower_factor.T)
```

```python
import functools

import jax
import jax.numpy as jnp
from jax import lax
from jax.experimental import pallas as pl
from jax.experimental.pallas import tpu as pltpu
from jax.sharding import PartitionSpec as P

MESH = pl.DeviceIdType.MESH
HIGHEST = lax.Precision.HIGHEST
VECTORS = 32
AMPS = 16384
TOTAL = 2097152
SITES = 21
SCALE = 4.0 / SITES
CHUNKS = 16
WIDTH = AMPS // CHUNKS
TOPS = WIDTH // 128
LEAD = 2
LAST_LAG = 3


def far_kernel(
    field_ref, bond_ref, previous_hbm, current_hbm, filtered_hbm, gram_ref,
    current, previous, filtered, weights, direct, ring_z, ring_x, gram, first, second,
    load_sem, send_sem, relay_sem, direct_sem, z_sem, x_sem, small_send, first_sem, second_sem,
):
    hi = lax.axis_index("hi")
    lo = lax.axis_index("lo")
    core = lo & 1
    z = lo >> 1
    x = hi & 3
    y = hi >> 2
    z0, z1, x0, x1, y0, y1 = z & 1, z >> 1, x & 1, x >> 1, y & 1, y >> 1

    load_current = pltpu.make_async_copy(current_hbm, current, load_sem.at[0])
    load_previous = pltpu.make_async_copy(previous_hbm, previous, load_sem.at[1])
    load_current.start()
    load_previous.start()

    barrier = pltpu.get_barrier_semaphore()
    for i in range(1, 8):
        pl.semaphore_signal(barrier, inc=1, device_id=(hi, lo ^ i), device_id_type=MESH)
    for i in range(1, 16):
        pl.semaphore_signal(barrier, inc=1, device_id=(hi ^ i, lo), device_id_type=MESH)
    pl.semaphore_wait(barrier, 22)

    def columns(k):
        return pl.ds(pl.multiple_of(k * WIDTH, WIDTH), WIDTH)

    partners = [(hi, lo ^ 1), (hi, lo ^ 3), (hi, lo ^ 6), (hi ^ 3, lo), (hi ^ 12, lo)]
    takes = [None, core != z0, z0 != z1, x0 != x1, y0 != y1]

    def when(condition, body):
        if condition is None:
            body()
        else:
            pl.when(condition)(body)

    def direct_copy(i, cols, sem):
        return pltpu.make_async_remote_copy(
            src_ref=current_hbm.at[:, cols], dst_ref=direct.at[i, :, cols],
            send_sem=send_sem.at[i], recv_sem=sem, device_id=partners[i], device_id_type=MESH,
        )

    first_path = core == 0

    def ring_plan(spot, pair_bit, ring_device, pair_device):
        role = jnp.where(pair_bit == 1, spot, 3 - spot)

        def at_role(r):
            return ring_device(jnp.where(pair_bit == 1, r, 3 - r))

        def pick(condition, a, b):
            return tuple(jnp.where(condition, u, v) for u, v in zip(a, b))

        own_device = pick(first_path, at_role(jnp.where(role == 0, 3, 0)), pair_device)
        last_a = jnp.where(first_path, 2, 0)
        last_b = jnp.where(first_path, 0, 2)
        has_a = (role == 3) | (role == last_a)
        has_b = (role == 3) | (role == last_b)
        a_device = pick(
            first_path,
            pick(role == 3, at_role(2), pair_device),
            pick(role == 3, at_role(0), at_role(1)),
        )
        b_device = pick(
            first_path,
            pick(role == 3, pair_device, at_role(3)),
            pick(role == 3, at_role(0), at_role(3)),
        )
        return dict(
            active=role < 2, own=(own_device, jnp.where(role == 0, 0, 1)),
            relays=[
                (has_a, a_device, jnp.where(role == 3, 0, 2), jnp.where(role == 3, 1, 2)),
                (has_b, b_device, jnp.where(role == 3, 2, 1), jnp.where(role == 3, 2, 1)),
            ],
        )

    plans = [
        (ring_z, z_sem, 5, 0, ring_plan(z, x0, lambda s: (hi, s * 2 + core), (hi ^ 1, lo))),
        (ring_x, x_sem, 6, 2, ring_plan(x, y0, lambda s: (y * 4 + s, lo), (hi ^ 4, lo))),
    ]

    def own_copy(ring, k_cols, sem_index, plan, recv):
        device, slot = plan["own"]
        return pltpu.make_async_remote_copy(
            src_ref=current_hbm.at[:, k_cols], dst_ref=ring.at[slot, :, k_cols],
            send_sem=send_sem.at[sem_index], recv_sem=recv, device_id=device, device_id_type=MESH,
        )

    def relay_copy(ring, which, k_cols, sem_index, relay, recv):
        _, device, slot, _ = relay
        return pltpu.make_async_remote_copy(
            src_ref=ring.at[which, :, k_cols], dst_ref=ring.at[slot, :, k_cols],
            send_sem=relay_sem.at[sem_index], recv_sem=recv, device_id=device, device_id_type=MESH,
        )

    def arrived(ring, slot, sems, k):
        cols = columns(k)
        pltpu.make_async_remote_copy(
            src_ref=ring.at[slot, :, cols], dst_ref=ring.at[slot, :, cols],
            send_sem=relay_sem.at[0], recv_sem=sems.at[slot, k],
            device_id=(hi, lo ^ 1), device_id_type=MESH,
        ).wait_recv()

    def send_own(k):
        cols = columns(k)
        for ring, sems, index, _, plan in plans:
            slot = plan["own"][1]
            when(plan["active"], lambda ring=ring, sems=sems, index=index, plan=plan, slot=slot:
                 own_copy(ring, cols, index, plan, sems.at[slot, k]).start())
        when(takes[1], lambda: direct_copy(1, cols, direct_sem.at[1, k]).start())

    @pl.loop(0, LEAD)
    def _(k):
        send_own(k)

    @pl.loop(0, CHUNKS)
    def _(k):
        cols = columns(k)
        for i in (2, 3, 4, 0):
            when(takes[i], lambda i=i: direct_copy(i, cols, direct_sem.at[i, k]).start())

    level = [bond_ref[s].astype(jnp.float32) for s in range(SITES - 1)]
    field = [0.75 * field_ref[s].astype(jnp.float32) for s in range(SITES)]
    half = [0.25 * v for v in level]
    full = [0.5 * v for v in level]

    def spin(bit):
        return 0.5 - bit.astype(jnp.float32)

    rows = lax.broadcasted_iota(jnp.int32, (128, 128), 0)
    lanes = lax.broadcasted_iota(jnp.int32, (128, 128), 1)
    flips = jnp.zeros((128, 128), jnp.float32)
    for s in range(7, 13):
        b = s - 7
        hit = (((lanes >> b) ^ (lanes >> (b + 1))) & 1 == 1) & (rows == lanes ^ (3 << b))
        flips = flips + jnp.where(hit, half[s], 0.0)
    lane_diagonal = jnp.zeros((128, 128), jnp.float32)
    for s in range(7, 14):
        lane_diagonal = lane_diagonal + field[s] * spin(lanes >> (s - 7) & 1)
        if s < 13:
            lane_diagonal = lane_diagonal + full[s] * spin(lanes >> (s - 7) & 1) * spin(
                lanes >> (s - 6) & 1
            )
    lane_diagonal = lane_diagonal + full[13] * spin(core) * spin(lanes >> 6 & 1)
    for top in range(2):
        seam = lane_diagonal + full[6] * (0.5 - top) * spin(lanes & 1)
        weights[top, 0:128, :] = flips + jnp.where(rows == lanes, seam, 0.0)
        hit = (rows == lanes ^ 1) & (lanes & 1 != top)
        weights[top, 128:256, :] = jnp.where(hit, half[6], 0.0)
    bits = [core, z0, z1, x0, x1, y0, y1]
    device_part = field[20] * spin(y1)
    for i in range(6):
        device_part = device_part + field[14 + i] * spin(bits[i])
        device_part = device_part + full[14 + i] * spin(bits[i]) * spin(bits[i + 1])

    lane = lax.broadcasted_iota(jnp.int32, (VECTORS, WIDTH), 1)
    core_factor = jnp.where((lane >> 6 & 1) != core, SCALE * half[13], 0.0)
    gram[...] = jnp.zeros_like(gram)

    def top_columns(t):
        return pl.ds(pl.multiple_of(t * 128, 128), 128)

    def local_part(k):
        sums = []
        left = []
        for i in range(TOPS):
            t = k * TOPS + i
            spins = [spin(t >> s & 1) for s in range(7)]
            diagonal = device_part + field[6] * spins[6]
            for s in range(6):
                diagonal = diagonal + field[s] * spins[s] + full[s] * spins[s] * spins[s + 1]
            own = current[:, top_columns(t)]
            total = diagonal * own
            for s in range(6):
                differ = ((t >> s) ^ (t >> (s + 1)) & 1) & 1
                factor = half[s] * differ.astype(jnp.float32)
                total = total + factor * current[:, top_columns(t ^ (3 << s))]
            sums.append(total)
            left.append(jnp.concatenate([own, current[:, top_columns(t ^ 64)]], axis=1))
        product = jnp.dot(
            jnp.concatenate(left, axis=0), weights[k // (CHUNKS // 2)],
            precision=HIGHEST, preferred_element_type=jnp.float32,
        )
        for i in range(TOPS):
            where = top_columns(k * TOPS + i)
            filtered[:, where] = (
                SCALE * (sums[i] + product[i * VECTORS:(i + 1) * VECTORS]) - previous[:, where]
            )

    def consume(k):
        cols = columns(k)

        direct_copy(0, cols, direct_sem.at[0, k]).wait_recv()
        filtered[:, cols] += core_factor * jnp.concatenate(
            [
                pltpu.roll(direct[0, :, top_columns(k * TOPS + i)], 64, 1)
                for i in range(TOPS)
            ],
            axis=1,
        )
        for i, bond in ((1, 14), (2, 15), (3, 17), (4, 19)):
            def add(i=i, bond=bond):
                direct_copy(i, cols, direct_sem.at[i, k]).wait_recv()
                filtered[:, cols] += SCALE * half[bond] * direct[i, :, cols]
            when(takes[i], add)
        for (ring, sems, _, _, plan), bond in zip(plans, (16, 18)):
            def add(ring=ring, sems=sems, bond=bond):
                arrived(ring, 2, sems, k)
                filtered[:, cols] += SCALE * half[bond] * ring[2, :, cols]
            when(plan["active"], add)
        part = filtered[:, cols]
        gram[...] += lax.dot_general(
            part, part, (((1,), (1,)), ((), ())), precision=HIGHEST,
            preferred_element_type=jnp.float32,
        )

    load_current.wait()
    load_previous.wait()

    @pl.loop(0, CHUNKS + LAST_LAG)
    def _(s):
        @pl.when(s + LEAD < CHUNKS)
        def _():
            send_own(s + LEAD)

        for ring, sems, _, base, plan in plans:
            for which in range(2):
                relay = plan["relays"][which]
                has, _, slot, lag = relay
                k = s - lag

                @pl.when(has & (k >= 0) & (k < CHUNKS))
                def _(ring=ring, sems=sems, base=base, which=which, relay=relay, slot=slot, k=k):
                    arrived(ring, which, sems, k)
                    relay_copy(
                        ring, which, columns(k), base + which, relay, sems.at[slot, k]
                    ).start()

        @pl.when(s < CHUNKS)
        def _():
            local_part(s)

        @pl.when(s >= LAST_LAG)
        def _():
            consume(s - LAST_LAG)

    store = pltpu.make_async_copy(filtered, filtered_hbm, load_sem.at[0])
    store.start()

    g = gram[...]
    packed = jnp.concatenate([g[8 * i:8 * i + 8, :] for i in range(4)], axis=1)
    for size, spot, box, sems, base, device in (
        (8, lo, first, first_sem, 0, lambda i: (hi, lo ^ i)),
        (16, hi, second, second_sem, 8, lambda i: (hi ^ i, lo)),
    ):
        box[spot] = packed

        def small(i):
            return pltpu.make_async_remote_copy(
                src_ref=box.at[spot], dst_ref=box.at[spot], send_sem=small_send.at[base + i],
                recv_sem=sems.at[spot], device_id=device(i), device_id_type=MESH,
            )

        for i in range(1, size):
            small(i).start()
        for i in range(1, size):
            other = spot ^ i
            pltpu.make_async_remote_copy(
                src_ref=box.at[other], dst_ref=box.at[other], send_sem=small_send.at[base + i],
                recv_sem=sems.at[other], device_id=device(i), device_id_type=MESH,
            ).wait_recv()
        packed = box[0]
        for i in range(1, size):
            packed = packed + box[i]
    gram_ref[...] = packed * (1.0 / TOTAL)

    whole = pl.ds(0, AMPS)
    for i in range(5):
        when(takes[i], lambda i=i: direct_copy(i, whole, direct_sem.at[i, 0]).wait_send())
    for ring, sems, index, base, plan in plans:
        when(plan["active"], lambda ring=ring, sems=sems, index=index, plan=plan:
             own_copy(ring, whole, index, plan, sems.at[0, 0]).wait_send())
        for which in range(2):
            relay = plan["relays"][which]
            when(relay[0], lambda ring=ring, sems=sems, base=base, which=which, relay=relay:
                 relay_copy(ring, which, whole, base + which, relay, sems.at[0, 0]).wait_send())
    for size, spot, box, sems, base, device in (
        (8, lo, first, first_sem, 0, lambda i: (hi, lo ^ i)),
        (16, hi, second, second_sem, 8, lambda i: (hi ^ i, lo)),
    ):
        for i in range(1, size):
            pltpu.make_async_remote_copy(
                src_ref=box.at[spot], dst_ref=box.at[spot], send_sem=small_send.at[base + i],
                recv_sem=sems.at[spot], device_id=device(i), device_id_type=MESH,
            ).wait_send()
    store.wait()


def last_kernel(gram_ref, filtered_ref, ortho_ref, upper_ref, inverse_ref):
    @pl.when(pl.program_id(0) == 0)
    def _():
        packed = gram_ref[...]
        parts = [packed] + [pltpu.roll(packed, 128 - 32 * i, 1) for i in range(1, 4)]
        table = jnp.concatenate(parts, axis=0)
        row = lax.broadcasted_iota(jnp.int32, (VECTORS, 128), 0)
        lane = lax.broadcasted_iota(jnp.int32, (VECTORS, 128), 1)
        table = jnp.where(lane < 32, table, jnp.where(lane - 32 == row, 1.0, 0.0))
        for j in range(VECTORS - 1):
            factor = table[:, j:j + 1] / table[j:j + 1, j:j + 1]
            factor = jnp.where(row[:, 0:1] > j, factor, 0.0)
            table = table - factor * table[j:j + 1, :]
        pivots = jnp.sum(jnp.where(row == lane, table, 0.0), axis=1, keepdims=True)
        table = table / jnp.sqrt(pivots)
        upper_ref[...] = jnp.where(lane >= row, table, 0.0)[:, 0:32]
        inverse_ref[...] = pltpu.roll(table, 96, 1)[:, 0:32]

    ortho_ref[...] = jnp.dot(
        inverse_ref[...], filtered_ref[...], precision=HIGHEST, preferred_element_type=jnp.float32
    )


def local(previous, current, field_levels, bond_levels):
    any_space = pl.BlockSpec(memory_space=pl.ANY)
    block = (VECTORS, AMPS)
    f32 = jnp.float32
    filtered, gram = pl.pallas_call(
        far_kernel,
        out_shape=(jax.ShapeDtypeStruct(block, f32), jax.ShapeDtypeStruct((8, 128), f32)),
        in_specs=[
            pl.BlockSpec(memory_space=pltpu.SMEM), pl.BlockSpec(memory_space=pltpu.SMEM),
            any_space, any_space,
        ],
        out_specs=(any_space, pl.BlockSpec(memory_space=pltpu.VMEM)),
        scratch_shapes=[
            pltpu.VMEM(block, f32), pltpu.VMEM(block, f32), pltpu.VMEM(block, f32),
            pltpu.VMEM((2, 256, 128), f32),
            pltpu.VMEM((5,) + block, f32), pltpu.VMEM((3,) + block, f32),
            pltpu.VMEM((3,) + block, f32),
            pltpu.VMEM((VECTORS, VECTORS), f32),
            pltpu.VMEM((8, 8, 128), f32), pltpu.VMEM((16, 8, 128), f32),
            pltpu.SemaphoreType.DMA((2,)), pltpu.SemaphoreType.DMA((7,)),
            pltpu.SemaphoreType.DMA((4,)), pltpu.SemaphoreType.DMA((5, CHUNKS)),
            pltpu.SemaphoreType.DMA((3, CHUNKS)), pltpu.SemaphoreType.DMA((3, CHUNKS)),
            pltpu.SemaphoreType.DMA((24,)), pltpu.SemaphoreType.DMA((8,)),
            pltpu.SemaphoreType.DMA((16,)),
        ],
        compiler_params=pltpu.CompilerParams(
            collective_id=1, has_side_effects=True, vmem_limit_bytes=44 << 20
        ),
        name="far_and_gram",
    )(field_levels, bond_levels, previous, current)
    tile = 2048
    return tuple(
        pl.pallas_call(
            last_kernel,
            grid=(AMPS // tile,),
            out_shape=(jax.ShapeDtypeStruct(block, f32), jax.ShapeDtypeStruct((32, 32), f32)),
            in_specs=[
                pl.BlockSpec((8, 128), lambda i: (0, 0)),
                pl.BlockSpec((VECTORS, tile), lambda i: (0, i)),
            ],
            out_specs=(
                pl.BlockSpec((VECTORS, tile), lambda i: (0, i)),
                pl.BlockSpec((32, 32), lambda i: (0, 0)),
            ),
            scratch_shapes=[pltpu.VMEM((32, 32), f32)],
            name="factor_and_apply",
        )(gram, filtered)
    )


def solution(mesh):
    in_specs = (P(None, ("hi", "lo")), P(None, ("hi", "lo")), P(), P())
    out_specs = (P(None, ("hi", "lo")), P())
    return jax.shard_map(local, mesh=mesh, in_specs=in_specs, out_specs=out_specs, check_vma=False)
```

```python
import functools

import jax
import jax.numpy as jnp
from jax import lax
from jax.experimental import pallas as pl
from jax.experimental.pallas import tpu as pltpu
from jax.sharding import PartitionSpec as P

MESH = pl.DeviceIdType.MESH
HIGHEST = lax.Precision.HIGHEST
VECTORS = 32
AMPS = 16384
TOTAL = 2097152
SITES = 21
SCALE = 4.0 / SITES
CHUNKS = 16
HOP = 2
WIDTH = AMPS // CHUNKS
TOPS = WIDTH // 128
LAST_LAG = 3 * HOP
TILES = 4
VMEM_LIMIT = 66000000


def far_kernel(
    field_hbm, bond_hbm, previous_hbm, current_hbm, filtered_hbm, gram_ref,
    field_ref, bond_ref, current, previous, filtered, weights, direct, ring_z, ring_x, gram, first, second,
    load_sem, send_sem, relay_sem, direct_sem, z_sem, x_sem, small_send, first_sem, second_sem,
):
    hi = lax.axis_index("hi")
    lo = lax.axis_index("lo")
    core = lo & 1
    z = lo >> 1
    x = hi & 3
    y = hi >> 2
    z0, z1, x0, x1, y0, y1 = z & 1, z >> 1, x & 1, x >> 1, y & 1, y >> 1

    load_current = pltpu.make_async_copy(current_hbm, current, load_sem.at[0])
    load_previous = pltpu.make_async_copy(previous_hbm, previous, load_sem.at[1])
    load_field = pltpu.make_async_copy(field_hbm, field_ref, load_sem.at[2])
    load_bond = pltpu.make_async_copy(bond_hbm, bond_ref, load_sem.at[3])
    load_field.start()
    load_bond.start()
    load_current.start()
    load_previous.start()

    barrier = pltpu.get_barrier_semaphore()
    for i in range(1, 8):
        pl.semaphore_signal(barrier, inc=1, device_id=(hi, lo ^ i), device_id_type=MESH)
    for i in range(1, 16):
        pl.semaphore_signal(barrier, inc=1, device_id=(hi ^ i, lo), device_id_type=MESH)
    pl.semaphore_wait(barrier, 22)

    def columns(k):
        return pl.ds(pl.multiple_of(k * WIDTH, WIDTH), WIDTH)

    partners = [(hi, lo ^ 1), (hi, lo ^ 3), (hi, lo ^ 6), (hi ^ 3, lo), (hi ^ 12, lo)]
    takes = [None, core != z0, z0 != z1, x0 != x1, y0 != y1]

    def when(condition, body):
        if condition is None:
            body()
        else:
            pl.when(condition)(body)

    def direct_copy(i, cols, sem):
        return pltpu.make_async_remote_copy(
            src_ref=current_hbm.at[:, cols], dst_ref=direct.at[i, :, cols],
            send_sem=send_sem.at[i], recv_sem=sem, device_id=partners[i], device_id_type=MESH,
        )

    first_path = core == 0

    def ring_plan(spot, pair_bit, ring_device, pair_device):
        role = jnp.where(pair_bit == 1, spot, 3 - spot)

        def at_role(r):
            return ring_device(jnp.where(pair_bit == 1, r, 3 - r))

        def pick(condition, a, b):
            return tuple(jnp.where(condition, u, v) for u, v in zip(a, b))

        own_device = pick(first_path, at_role(jnp.where(role == 0, 3, 0)), pair_device)
        last_a = jnp.where(first_path, 2, 0)
        last_b = jnp.where(first_path, 0, 2)
        has_a = (role == 3) | (role == last_a)
        has_b = (role == 3) | (role == last_b)
        a_device = pick(
            first_path,
            pick(role == 3, at_role(2), pair_device),
            pick(role == 3, at_role(0), at_role(1)),
        )
        b_device = pick(
            first_path,
            pick(role == 3, pair_device, at_role(3)),
            pick(role == 3, at_role(0), at_role(3)),
        )
        return dict(
            active=role < 2, own=(own_device, jnp.where(role == 0, 0, 1)),
            relays=[
                (has_a, a_device, jnp.where(role == 3, 0, 2), jnp.where(role == 3, HOP, 2 * HOP)),
                (has_b, b_device, jnp.where(role == 3, 2, 1), jnp.where(role == 3, 2 * HOP, HOP)),
            ],
        )

    plans = [
        (ring_z, z_sem, 5, 0, ring_plan(z, x0, lambda s: (hi, s * 2 + core), (hi ^ 1, lo))),
        (ring_x, x_sem, 6, 2, ring_plan(x, y0, lambda s: (y * 4 + s, lo), (hi ^ 4, lo))),
    ]

    def own_copy(ring, k_cols, sem_index, plan, recv):
        device, slot = plan["own"]
        return pltpu.make_async_remote_copy(
            src_ref=current_hbm.at[:, k_cols], dst_ref=ring.at[slot, :, k_cols],
            send_sem=send_sem.at[sem_index], recv_sem=recv, device_id=device, device_id_type=MESH,
        )

    def relay_copy(ring, which, k_cols, sem_index, relay, recv):
        _, device, slot, _ = relay
        return pltpu.make_async_remote_copy(
            src_ref=ring.at[which, :, k_cols], dst_ref=ring.at[slot, :, k_cols],
            send_sem=relay_sem.at[sem_index], recv_sem=recv, device_id=device, device_id_type=MESH,
        )

    def arrived(ring, slot, sems, k):
        cols = columns(k)
        pltpu.make_async_remote_copy(
            src_ref=ring.at[slot, :, cols], dst_ref=ring.at[slot, :, cols],
            send_sem=relay_sem.at[0], recv_sem=sems.at[slot, k],
            device_id=(hi, lo ^ 1), device_id_type=MESH,
        ).wait_recv()

    def send_own(k):
        cols = columns(k)
        for ring, sems, index, _, plan in plans:
            slot = plan["own"][1]
            when(plan["active"], lambda ring=ring, sems=sems, index=index, plan=plan, slot=slot:
                 own_copy(ring, cols, index, plan, sems.at[slot, k]).start())
        for i in (1, 2, 3, 4, 0):
            when(takes[i], lambda i=i: direct_copy(i, cols, direct_sem.at[i, k]).start())

    load_field.wait()
    load_bond.wait()
    level = [bond_ref[s].astype(jnp.float32) for s in range(SITES - 1)]
    field = [0.75 * field_ref[s].astype(jnp.float32) for s in range(SITES)]
    half = [0.25 * v for v in level]
    full = [0.5 * v for v in level]

    def spin(bit):
        return 0.5 - bit.astype(jnp.float32)

    rows = lax.broadcasted_iota(jnp.int32, (128, 128), 0)
    lanes = lax.broadcasted_iota(jnp.int32, (128, 128), 1)
    flips = jnp.zeros((128, 128), jnp.float32)
    for s in range(7, 13):
        b = s - 7
        hit = (((lanes >> b) ^ (lanes >> (b + 1))) & 1 == 1) & (rows == lanes ^ (3 << b))
        flips = flips + jnp.where(hit, half[s], 0.0)
    lane_diagonal = jnp.zeros((128, 128), jnp.float32)
    for s in range(7, 14):
        lane_diagonal = lane_diagonal + field[s] * spin(lanes >> (s - 7) & 1)
        if s < 13:
            lane_diagonal = lane_diagonal + full[s] * spin(lanes >> (s - 7) & 1) * spin(
                lanes >> (s - 6) & 1
            )
    lane_diagonal = lane_diagonal + full[13] * spin(core) * spin(lanes >> 6 & 1)
    for top in range(2):
        seam = lane_diagonal + full[6] * (0.5 - top) * spin(lanes & 1)
        weights[top, 0:128, :] = flips + jnp.where(rows == lanes, seam, 0.0)
        hit = (rows == lanes ^ 1) & (lanes & 1 != top)
        weights[top, 128:256, :] = jnp.where(hit, half[6], 0.0)
    bits = [core, z0, z1, x0, x1, y0, y1]
    device_part = field[20] * spin(y1)
    for i in range(6):
        device_part = device_part + field[14 + i] * spin(bits[i])
        device_part = device_part + full[14 + i] * spin(bits[i]) * spin(bits[i + 1])

    lane = lax.broadcasted_iota(jnp.int32, (VECTORS, WIDTH), 1)
    core_factor = jnp.where((lane >> 6 & 1) != core, SCALE * half[13], 0.0)
    gram[...] = jnp.zeros_like(gram)

    def top_columns(t):
        return pl.ds(pl.multiple_of(t * 128, 128), 128)

    def local_part(k):
        sums = []
        left = []
        for i in range(TOPS):
            t = k * TOPS + i
            spins = [spin(t >> s & 1) for s in range(7)]
            diagonal = device_part + field[6] * spins[6]
            for s in range(6):
                diagonal = diagonal + field[s] * spins[s] + full[s] * spins[s] * spins[s + 1]
            own = current[:, top_columns(t)]
            total = diagonal * own
            for s in range(6):
                differ = ((t >> s) ^ (t >> (s + 1)) & 1) & 1
                factor = half[s] * differ.astype(jnp.float32)
                total = total + factor * current[:, top_columns(t ^ (3 << s))]
            sums.append(total)
            left.append(jnp.concatenate([own, current[:, top_columns(t ^ 64)]], axis=1))
        product = jnp.dot(
            jnp.concatenate(left, axis=0), weights[k // (CHUNKS // 2)],
            precision=HIGHEST, preferred_element_type=jnp.float32,
        )
        for i in range(TOPS):
            where = top_columns(k * TOPS + i)
            filtered[:, where] = (
                SCALE * (sums[i] + product[i * VECTORS:(i + 1) * VECTORS]) - previous[:, where]
            )

    def consume(k):
        cols = columns(k)

        direct_copy(0, cols, direct_sem.at[0, k]).wait_recv()
        filtered[:, cols] += core_factor * jnp.concatenate(
            [
                pltpu.roll(direct[0, :, top_columns(k * TOPS + i)], 64, 1)
                for i in range(TOPS)
            ],
            axis=1,
        )
        for i, bond in ((1, 14), (2, 15), (3, 17), (4, 19)):
            def add(i=i, bond=bond):
                direct_copy(i, cols, direct_sem.at[i, k]).wait_recv()
                filtered[:, cols] += SCALE * half[bond] * direct[i, :, cols]
            when(takes[i], add)
        for (ring, sems, _, _, plan), bond in zip(plans, (16, 18)):
            def add(ring=ring, sems=sems, bond=bond):
                arrived(ring, 2, sems, k)
                filtered[:, cols] += SCALE * half[bond] * ring[2, :, cols]
            when(plan["active"], add)
        part = filtered[:, cols]
        gram[...] += lax.dot_general(
            part, part, (((1,), (1,)), ((), ())), precision=HIGHEST,
            preferred_element_type=jnp.float32,
        )

    load_current.wait()
    load_previous.wait()

    @pl.loop(0, CHUNKS + LAST_LAG)
    def _(s):
        @pl.when(s < CHUNKS)
        def _():
            send_own(s)

        for ring, sems, _, base, plan in plans:
            for which in range(2):
                relay = plan["relays"][which]
                has, _, slot, lag = relay
                k = s - lag

                @pl.when(has & (k >= 0) & (k < CHUNKS))
                def _(ring=ring, sems=sems, base=base, which=which, relay=relay, slot=slot, k=k):
                    arrived(ring, which, sems, k)
                    relay_copy(
                        ring, which, columns(k), base + which, relay, sems.at[slot, k]
                    ).start()

        @pl.when(s < CHUNKS)
        def _():
            local_part(s)

        @pl.when(s >= LAST_LAG)
        def _():
            consume(s - LAST_LAG)

    store = pltpu.make_async_copy(filtered, filtered_hbm, load_sem.at[0])
    store.start()

    g = gram[...]
    packed = jnp.concatenate([g[8 * i:8 * i + 8, :] for i in range(4)], axis=1)
    for size, spot, box, sems, base, device in (
        (8, lo, first, first_sem, 0, lambda i: (hi, lo ^ i)),
        (16, hi, second, second_sem, 8, lambda i: (hi ^ i, lo)),
    ):
        box[spot] = packed

        def small(i):
            return pltpu.make_async_remote_copy(
                src_ref=box.at[spot], dst_ref=box.at[spot], send_sem=small_send.at[base + i],
                recv_sem=sems.at[spot], device_id=device(i), device_id_type=MESH,
            )

        for i in range(1, size):
            small(i).start()
        for i in range(1, size):
            other = spot ^ i
            pltpu.make_async_remote_copy(
                src_ref=box.at[other], dst_ref=box.at[other], send_sem=small_send.at[base + i],
                recv_sem=sems.at[other], device_id=device(i), device_id_type=MESH,
            ).wait_recv()
        packed = box[0]
        for i in range(1, size):
            packed = packed + box[i]
    gram_ref[...] = packed * (1.0 / TOTAL)

    whole = pl.ds(0, AMPS)
    for i in range(5):
        when(takes[i], lambda i=i: direct_copy(i, whole, direct_sem.at[i, 0]).wait_send())
    for ring, sems, index, base, plan in plans:
        when(plan["active"], lambda ring=ring, sems=sems, index=index, plan=plan:
             own_copy(ring, whole, index, plan, sems.at[0, 0]).wait_send())
        for which in range(2):
            relay = plan["relays"][which]
            when(relay[0], lambda ring=ring, sems=sems, base=base, which=which, relay=relay:
                 relay_copy(ring, which, whole, base + which, relay, sems.at[0, 0]).wait_send())
    for size, spot, box, sems, base, device in (
        (8, lo, first, first_sem, 0, lambda i: (hi, lo ^ i)),
        (16, hi, second, second_sem, 8, lambda i: (hi ^ i, lo)),
    ):
        for i in range(1, size):
            pltpu.make_async_remote_copy(
                src_ref=box.at[spot], dst_ref=box.at[spot], send_sem=small_send.at[base + i],
                recv_sem=sems.at[spot], device_id=device(i), device_id_type=MESH,
            ).wait_send()
    store.wait()


def last_kernel(gram_ref, filtered_hbm, ortho_hbm, upper_ref, filtered, ortho, load_sem, store_sem):
    tile = AMPS // TILES

    def load(i):
        cols = pl.ds(i * tile, tile)
        return pltpu.make_async_copy(filtered_hbm.at[:, cols], filtered.at[:, cols], load_sem.at[i])

    def store(i):
        cols = pl.ds(i * tile, tile)
        return pltpu.make_async_copy(ortho.at[:, cols], ortho_hbm.at[:, cols], store_sem.at[i])

    for i in range(TILES):
        load(i).start()

    packed = gram_ref[...]
    parts = [packed] + [pltpu.roll(packed, 128 - 32 * i, 1) for i in range(1, 4)]
    table = jnp.concatenate(parts, axis=0)
    row = lax.broadcasted_iota(jnp.int32, (VECTORS, 128), 0)
    lane = lax.broadcasted_iota(jnp.int32, (VECTORS, 128), 1)
    table = jnp.where(lane < 32, table, jnp.where(lane - 32 == row, 1.0, 0.0))
    for j in range(VECTORS - 1):
        factor = table[:, j:j + 1] / table[j:j + 1, j:j + 1]
        factor = jnp.where(row[:, 0:1] > j, factor, 0.0)
        table = table - factor * table[j:j + 1, :]
    pivots = jnp.sum(jnp.where(row == lane, table, 0.0), axis=1, keepdims=True)
    table = table / jnp.sqrt(pivots)
    upper_ref[...] = jnp.where(lane >= row, table, 0.0)[:, 0:32]
    inverse = pltpu.roll(table, 96, 1)[:, 0:32]

    def split(values):
        high = values.astype(jnp.bfloat16)
        rest = values - high.astype(jnp.float32)
        middle = rest.astype(jnp.bfloat16)
        low = (rest - middle.astype(jnp.float32)).astype(jnp.bfloat16)
        return high, middle, low

    high, middle, low = split(inverse)
    none = jnp.zeros_like(high)
    left = jnp.concatenate(
        [
            jnp.concatenate([high, high, high], axis=1),
            jnp.concatenate([middle, middle, none], axis=1),
            jnp.concatenate([low, none, none], axis=1),
        ],
        axis=0,
    )
    for i in range(TILES):
        load(i).wait()
        cols = pl.ds(i * tile, tile)
        right = jnp.concatenate(split(filtered[:, cols]), axis=0)
        parts = jnp.dot(left, right, preferred_element_type=jnp.float32)
        ortho[:, cols] = parts[0:32] + (parts[32:64] + parts[64:96])
        store(i).start()
    for i in range(TILES):
        store(i).wait()


def local(previous, current, field_levels, bond_levels):
    hbm = pl.BlockSpec(memory_space=pltpu.HBM)
    block = (VECTORS, AMPS)
    f32 = jnp.float32
    filtered, gram = pl.pallas_call(
        far_kernel,
        out_shape=(jax.ShapeDtypeStruct(block, f32), jax.ShapeDtypeStruct((8, 128), f32)),
        in_specs=[
            hbm, hbm, hbm, hbm,
        ],
        out_specs=(hbm, pl.BlockSpec(memory_space=pltpu.VMEM)),
        scratch_shapes=[
            pltpu.SMEM((SITES,), jnp.int32), pltpu.SMEM((SITES - 1,), jnp.int32),
            pltpu.VMEM(block, f32), pltpu.VMEM(block, f32), pltpu.VMEM(block, f32),
            pltpu.VMEM((2, 256, 128), f32),
            pltpu.VMEM((5,) + block, f32), pltpu.VMEM((3,) + block, f32),
            pltpu.VMEM((3,) + block, f32),
            pltpu.VMEM((VECTORS, VECTORS), f32),
            pltpu.VMEM((8, 8, 128), f32), pltpu.VMEM((16, 8, 128), f32),
            pltpu.SemaphoreType.DMA((4,)), pltpu.SemaphoreType.DMA((7,)),
            pltpu.SemaphoreType.DMA((4,)), pltpu.SemaphoreType.DMA((5, CHUNKS)),
            pltpu.SemaphoreType.DMA((3, CHUNKS)), pltpu.SemaphoreType.DMA((3, CHUNKS)),
            pltpu.SemaphoreType.DMA((24,)), pltpu.SemaphoreType.DMA((8,)),
            pltpu.SemaphoreType.DMA((16,)),
        ],
        compiler_params=pltpu.CompilerParams(
            collective_id=1, has_side_effects=True, vmem_limit_bytes=VMEM_LIMIT
        ),
        name="far_and_gram",
    )(field_levels, bond_levels, previous, current)
    return tuple(
        pl.pallas_call(
            last_kernel,
            out_shape=(jax.ShapeDtypeStruct(block, f32), jax.ShapeDtypeStruct((32, 32), f32)),
            in_specs=[pl.BlockSpec(memory_space=pltpu.VMEM), hbm],
            out_specs=(hbm, pl.BlockSpec(memory_space=pltpu.VMEM)),
            scratch_shapes=[
                pltpu.VMEM(block, f32), pltpu.VMEM(block, f32),
                pltpu.SemaphoreType.DMA((TILES,)), pltpu.SemaphoreType.DMA((TILES,)),
            ],
            compiler_params=pltpu.CompilerParams(vmem_limit_bytes=VMEM_LIMIT),
            name="factor_and_apply",
        )(gram, filtered)
    )


def solution(mesh):
    in_specs = (P(None, ("hi", "lo")), P(None, ("hi", "lo")), P(), P())
    out_specs = (P(None, ("hi", "lo")), P())
    return jax.shard_map(local, mesh=mesh, in_specs=in_specs, out_specs=out_specs, check_vma=False)
```

```python
import functools

import jax
import jax.numpy as jnp
from jax import lax
from jax.experimental import pallas as pl
from jax.experimental.pallas import tpu as pltpu
from jax.sharding import PartitionSpec as P

MESH = pl.DeviceIdType.MESH
HIGHEST = lax.Precision.HIGHEST
VECTORS = 32
AMPS = 16384
TOTAL = 2097152
SITES = 21
SCALE = 4.0 / SITES
CHUNKS = 16
HOP = 2
WIDTH = AMPS // CHUNKS
TOPS = WIDTH // 128
LAST_LAG = 3 * HOP
TILES = 4
VMEM_LIMIT = 66000000


def far_kernel(
    field_hbm, bond_hbm, previous_hbm, current_hbm, filtered_hbm, gram_ref,
    field_ref, bond_ref, current, previous, filtered, weights, direct, ring_z, ring_x, gram, first, second,
    load_sem, send_sem, relay_sem, direct_sem, z_sem, x_sem, small_send, first_sem, second_sem,
):
    hi = lax.axis_index("hi")
    lo = lax.axis_index("lo")
    core = lo & 1
    z = lo >> 1
    x = hi & 3
    y = hi >> 2
    z0, z1, x0, x1, y0, y1 = z & 1, z >> 1, x & 1, x >> 1, y & 1, y >> 1

    load_current = pltpu.make_async_copy(current_hbm, current, load_sem.at[0])
    load_previous = pltpu.make_async_copy(previous_hbm, previous, load_sem.at[1])
    load_field = pltpu.make_async_copy(field_hbm, field_ref, load_sem.at[2])
    load_bond = pltpu.make_async_copy(bond_hbm, bond_ref, load_sem.at[3])
    load_field.start()
    load_bond.start()
    load_current.start()
    load_previous.start()

    barrier = pltpu.get_barrier_semaphore()
    for i in range(1, 8):
        pl.semaphore_signal(barrier, inc=1, device_id=(hi, lo ^ i), device_id_type=MESH)
    for i in range(1, 16):
        pl.semaphore_signal(barrier, inc=1, device_id=(hi ^ i, lo), device_id_type=MESH)

    def columns(k):
        return pl.ds(pl.multiple_of(k * WIDTH, WIDTH), WIDTH)

    partners = [(hi, lo ^ 1), (hi, lo ^ 3), (hi, lo ^ 6), (hi ^ 3, lo), (hi ^ 12, lo)]
    takes = [None, core != z0, z0 != z1, x0 != x1, y0 != y1]

    def when(condition, body):
        if condition is None:
            body()
        else:
            pl.when(condition)(body)

    def direct_copy(i, cols, sem):
        return pltpu.make_async_remote_copy(
            src_ref=current_hbm.at[:, cols], dst_ref=direct.at[i, :, cols],
            send_sem=send_sem.at[i], recv_sem=sem, device_id=partners[i], device_id_type=MESH,
        )

    first_path = core == 0

    def ring_plan(spot, pair_bit, ring_device, pair_device):
        role = jnp.where(pair_bit == 1, spot, 3 - spot)

        def at_role(r):
            return ring_device(jnp.where(pair_bit == 1, r, 3 - r))

        def pick(condition, a, b):
            return tuple(jnp.where(condition, u, v) for u, v in zip(a, b))

        own_device = pick(first_path, at_role(jnp.where(role == 0, 3, 0)), pair_device)
        last_a = jnp.where(first_path, 2, 0)
        last_b = jnp.where(first_path, 0, 2)
        has_a = (role == 3) | (role == last_a)
        has_b = (role == 3) | (role == last_b)
        a_device = pick(
            first_path,
            pick(role == 3, at_role(2), pair_device),
            pick(role == 3, at_role(0), at_role(1)),
        )
        b_device = pick(
            first_path,
            pick(role == 3, pair_device, at_role(3)),
            pick(role == 3, at_role(0), at_role(3)),
        )
        return dict(
            active=role < 2, own=(own_device, jnp.where(role == 0, 0, 1)),
            relays=[
                (has_a, a_device, jnp.where(role == 3, 0, 2), jnp.where(role == 3, HOP, 2 * HOP)),
                (has_b, b_device, jnp.where(role == 3, 2, 1), jnp.where(role == 3, 2 * HOP, HOP)),
            ],
        )

    plans = [
        (ring_z, z_sem, 5, 0, ring_plan(z, x0, lambda s: (hi, s * 2 + core), (hi ^ 1, lo))),
        (ring_x, x_sem, 6, 2, ring_plan(x, y0, lambda s: (y * 4 + s, lo), (hi ^ 4, lo))),
    ]

    def own_copy(ring, k_cols, sem_index, plan, recv):
        device, slot = plan["own"]
        return pltpu.make_async_remote_copy(
            src_ref=current_hbm.at[:, k_cols], dst_ref=ring.at[slot, :, k_cols],
            send_sem=send_sem.at[sem_index], recv_sem=recv, device_id=device, device_id_type=MESH,
        )

    def relay_copy(ring, which, k_cols, sem_index, relay, recv):
        _, device, slot, _ = relay
        return pltpu.make_async_remote_copy(
            src_ref=ring.at[which, :, k_cols], dst_ref=ring.at[slot, :, k_cols],
            send_sem=relay_sem.at[sem_index], recv_sem=recv, device_id=device, device_id_type=MESH,
        )

    def arrived(ring, slot, sems, k):
        cols = columns(k)
        pltpu.make_async_remote_copy(
            src_ref=ring.at[slot, :, cols], dst_ref=ring.at[slot, :, cols],
            send_sem=relay_sem.at[0], recv_sem=sems.at[slot, k],
            device_id=(hi, lo ^ 1), device_id_type=MESH,
        ).wait_recv()

    def send_own(k):
        cols = columns(k)
        for i in (1, 2, 3, 4, 0):
            when(takes[i], lambda i=i: direct_copy(i, cols, direct_sem.at[i, k]).start())

    def send_ring(s):
        for ring, sems, index, _, plan in plans:
            slot = plan["own"][1]
            k = s

            @pl.when(plan["active"] & (k < CHUNKS))
            def _(ring=ring, sems=sems, index=index, plan=plan, slot=slot, k=k):
                own_copy(ring, columns(k), index, plan, sems.at[slot, k]).start()

    load_field.wait()
    load_bond.wait()
    level = [bond_ref[s].astype(jnp.float32) for s in range(SITES - 1)]
    field = [0.75 * field_ref[s].astype(jnp.float32) for s in range(SITES)]
    half = [0.25 * v for v in level]
    full = [0.5 * v for v in level]

    def spin(bit):
        return 0.5 - bit.astype(jnp.float32)

    rows = lax.broadcasted_iota(jnp.int32, (128, 128), 0)
    lanes = lax.broadcasted_iota(jnp.int32, (128, 128), 1)
    flips = jnp.zeros((128, 128), jnp.float32)
    for s in range(7, 13):
        b = s - 7
        hit = (((lanes >> b) ^ (lanes >> (b + 1))) & 1 == 1) & (rows == lanes ^ (3 << b))
        flips = flips + jnp.where(hit, half[s], 0.0)
    lane_diagonal = jnp.zeros((128, 128), jnp.float32)
    for s in range(7, 14):
        lane_diagonal = lane_diagonal + field[s] * spin(lanes >> (s - 7) & 1)
        if s < 13:
            lane_diagonal = lane_diagonal + full[s] * spin(lanes >> (s - 7) & 1) * spin(
                lanes >> (s - 6) & 1
            )
    lane_diagonal = lane_diagonal + full[13] * spin(core) * spin(lanes >> 6 & 1)
    for top in range(2):
        seam = lane_diagonal + full[6] * (0.5 - top) * spin(lanes & 1)
        weights[top, 0:128, :] = flips + jnp.where(rows == lanes, seam, 0.0)
        hit = (rows == lanes ^ 1) & (lanes & 1 != top)
        weights[top, 128:256, :] = jnp.where(hit, half[6], 0.0)
    bits = [core, z0, z1, x0, x1, y0, y1]
    device_part = field[20] * spin(y1)
    for i in range(6):
        device_part = device_part + field[14 + i] * spin(bits[i])
        device_part = device_part + full[14 + i] * spin(bits[i]) * spin(bits[i + 1])

    lane = lax.broadcasted_iota(jnp.int32, (VECTORS, WIDTH), 1)
    core_factor = jnp.where((lane >> 6 & 1) != core, SCALE * half[13], 0.0)
    gram[...] = jnp.zeros_like(gram)

    def top_columns(t):
        return pl.ds(pl.multiple_of(t * 128, 128), 128)

    def local_part(k):
        sums = []
        left = []
        for i in range(TOPS):
            t = k * TOPS + i
            spins = [spin(t >> s & 1) for s in range(7)]
            diagonal = device_part + field[6] * spins[6]
            for s in range(6):
                diagonal = diagonal + field[s] * spins[s] + full[s] * spins[s] * spins[s + 1]
            own = current[:, top_columns(t)]
            total = diagonal * own
            for s in range(6):
                differ = ((t >> s) ^ (t >> (s + 1)) & 1) & 1
                factor = half[s] * differ.astype(jnp.float32)
                total = total + factor * current[:, top_columns(t ^ (3 << s))]
            sums.append(total)
            left.append(jnp.concatenate([own, current[:, top_columns(t ^ 64)]], axis=1))
        product = jnp.dot(
            jnp.concatenate(left, axis=0), weights[k // (CHUNKS // 2)],
            precision=HIGHEST, preferred_element_type=jnp.float32,
        )
        for i in range(TOPS):
            where = top_columns(k * TOPS + i)
            filtered[:, where] = (
                SCALE * (sums[i] + product[i * VECTORS:(i + 1) * VECTORS]) - previous[:, where]
            )

    def consume(k):
        cols = columns(k)

        direct_copy(0, cols, direct_sem.at[0, k]).wait_recv()
        filtered[:, cols] += core_factor * jnp.concatenate(
            [
                pltpu.roll(direct[0, :, top_columns(k * TOPS + i)], 64, 1)
                for i in range(TOPS)
            ],
            axis=1,
        )
        for i, bond in ((1, 14), (2, 15), (3, 17), (4, 19)):
            def add(i=i, bond=bond):
                direct_copy(i, cols, direct_sem.at[i, k]).wait_recv()
                filtered[:, cols] += SCALE * half[bond] * direct[i, :, cols]
            when(takes[i], add)
        for (ring, sems, _, _, plan), bond in zip(plans, (16, 18)):
            def add(ring=ring, sems=sems, bond=bond):
                arrived(ring, 2, sems, k)
                filtered[:, cols] += SCALE * half[bond] * ring[2, :, cols]
            when(plan["active"], add)
        part = filtered[:, cols]
        gram[...] += lax.dot_general(
            part, part, (((1,), (1,)), ((), ())), precision=HIGHEST,
            preferred_element_type=jnp.float32,
        )

    pl.semaphore_wait(barrier, 22)

    @pl.loop(0, CHUNKS + LAST_LAG)
    def _(s):
        send_ring(s)

        @pl.when(s < CHUNKS)
        def _():
            send_own(s)

        for ring, sems, _, base, plan in plans:
            for which in range(2):
                relay = plan["relays"][which]
                has, _, slot, lag = relay
                k = s - lag

                @pl.when(has & (k >= 0) & (k < CHUNKS))
                def _(ring=ring, sems=sems, base=base, which=which, relay=relay, slot=slot, k=k):
                    arrived(ring, which, sems, k)
                    relay_copy(
                        ring, which, columns(k), base + which, relay, sems.at[slot, k]
                    ).start()

        @pl.when(s < CHUNKS)
        def _():
            @pl.when(s == 0)
            def _():
                load_current.wait()
                load_previous.wait()

            local_part(s)

        @pl.when(s >= LAST_LAG)
        def _():
            consume(s - LAST_LAG)

    store = pltpu.make_async_copy(filtered, filtered_hbm, load_sem.at[0])
    store.start()

    g = gram[...]
    packed = jnp.concatenate([g[8 * i:8 * i + 8, :] for i in range(4)], axis=1)
    for size, spot, box, sems, base, device in (
        (8, lo, first, first_sem, 0, lambda i: (hi, lo ^ i)),
        (16, hi, second, second_sem, 8, lambda i: (hi ^ i, lo)),
    ):
        box[spot] = packed

        def small(i):
            return pltpu.make_async_remote_copy(
                src_ref=box.at[spot], dst_ref=box.at[spot], send_sem=small_send.at[base + i],
                recv_sem=sems.at[spot], device_id=device(i), device_id_type=MESH,
            )

        for i in range(1, size):
            small(i).start()
        for i in range(1, size):
            other = spot ^ i
            pltpu.make_async_remote_copy(
                src_ref=box.at[other], dst_ref=box.at[other], send_sem=small_send.at[base + i],
                recv_sem=sems.at[other], device_id=device(i), device_id_type=MESH,
            ).wait_recv()
        packed = box[0]
        for i in range(1, size):
            packed = packed + box[i]
    gram_ref[...] = packed * (1.0 / TOTAL)

    whole = pl.ds(0, AMPS)
    for i in range(5):
        when(takes[i], lambda i=i: direct_copy(i, whole, direct_sem.at[i, 0]).wait_send())
    for ring, sems, index, base, plan in plans:
        when(plan["active"], lambda ring=ring, sems=sems, index=index, plan=plan:
             own_copy(ring, whole, index, plan, sems.at[0, 0]).wait_send())
        for which in range(2):
            relay = plan["relays"][which]
            when(relay[0], lambda ring=ring, sems=sems, base=base, which=which, relay=relay:
                 relay_copy(ring, which, whole, base + which, relay, sems.at[0, 0]).wait_send())
    for size, spot, box, sems, base, device in (
        (8, lo, first, first_sem, 0, lambda i: (hi, lo ^ i)),
        (16, hi, second, second_sem, 8, lambda i: (hi ^ i, lo)),
    ):
        for i in range(1, size):
            pltpu.make_async_remote_copy(
                src_ref=box.at[spot], dst_ref=box.at[spot], send_sem=small_send.at[base + i],
                recv_sem=sems.at[spot], device_id=device(i), device_id_type=MESH,
            ).wait_send()
    store.wait()


def last_kernel(
    gram_ref, filtered_hbm, ortho_hbm, upper_hbm, filtered, ortho, upper, load_sem, store_sem, upper_sem
):
    tile = AMPS // TILES

    def load(i):
        cols = pl.ds(i * tile, tile)
        return pltpu.make_async_copy(filtered_hbm.at[:, cols], filtered.at[:, cols], load_sem.at[i])

    def store(i):
        cols = pl.ds(i * tile, tile)
        return pltpu.make_async_copy(ortho.at[:, cols], ortho_hbm.at[:, cols], store_sem.at[i])

    for i in range(TILES):
        load(i).start()

    packed = gram_ref[...]
    parts = [packed] + [pltpu.roll(packed, 128 - 32 * i, 1) for i in range(1, 4)]
    table = jnp.concatenate(parts, axis=0)
    row = lax.broadcasted_iota(jnp.int32, (VECTORS, 128), 0)
    lane = lax.broadcasted_iota(jnp.int32, (VECTORS, 128), 1)
    table = jnp.where(lane < 32, table, jnp.where(lane - 32 == row, 1.0, 0.0))
    for j in range(VECTORS - 1):
        factor = table[:, j:j + 1] / table[j:j + 1, j:j + 1]
        factor = jnp.where(row[:, 0:1] > j, factor, 0.0)
        table = table - factor * table[j:j + 1, :]
    pivots = jnp.sum(jnp.where(row == lane, table, 0.0), axis=1, keepdims=True)
    table = table / jnp.sqrt(pivots)
    upper[...] = jnp.where(lane >= row, table, 0.0)[:, 0:32]
    store_upper = pltpu.make_async_copy(upper, upper_hbm, upper_sem)
    store_upper.start()
    inverse = pltpu.roll(table, 96, 1)[:, 0:32]

    def split(values):
        high = values.astype(jnp.bfloat16)
        rest = values - high.astype(jnp.float32)
        middle = rest.astype(jnp.bfloat16)
        low = (rest - middle.astype(jnp.float32)).astype(jnp.bfloat16)
        return high, middle, low

    high, middle, low = split(inverse)
    none = jnp.zeros_like(high)
    left = jnp.concatenate(
        [
            jnp.concatenate([high, high, high], axis=1),
            jnp.concatenate([middle, middle, none], axis=1),
            jnp.concatenate([low, none, none], axis=1),
        ],
        axis=0,
    )
    for i in range(TILES):
        load(i).wait()
        cols = pl.ds(i * tile, tile)
        right = jnp.concatenate(split(filtered[:, cols]), axis=0)
        parts = jnp.dot(left, right, preferred_element_type=jnp.float32)
        ortho[:, cols] = parts[0:32] + (parts[32:64] + parts[64:96])
        store(i).start()
    for i in range(TILES):
        store(i).wait()
    store_upper.wait()


def local(previous, current, field_levels, bond_levels):
    hbm = pl.BlockSpec(memory_space=pltpu.HBM)
    block = (VECTORS, AMPS)
    f32 = jnp.float32
    filtered, gram = pl.pallas_call(
        far_kernel,
        out_shape=(jax.ShapeDtypeStruct(block, f32), jax.ShapeDtypeStruct((8, 128), f32)),
        in_specs=[
            hbm, hbm, hbm, hbm,
        ],
        out_specs=(hbm, pl.BlockSpec(memory_space=pltpu.VMEM)),
        scratch_shapes=[
            pltpu.SMEM((SITES,), jnp.int32), pltpu.SMEM((SITES - 1,), jnp.int32),
            pltpu.VMEM(block, f32), pltpu.VMEM(block, f32), pltpu.VMEM(block, f32),
            pltpu.VMEM((2, 256, 128), f32),
            pltpu.VMEM((5,) + block, f32), pltpu.VMEM((3,) + block, f32),
            pltpu.VMEM((3,) + block, f32),
            pltpu.VMEM((VECTORS, VECTORS), f32),
            pltpu.VMEM((8, 8, 128), f32), pltpu.VMEM((16, 8, 128), f32),
            pltpu.SemaphoreType.DMA((4,)), pltpu.SemaphoreType.DMA((7,)),
            pltpu.SemaphoreType.DMA((4,)), pltpu.SemaphoreType.DMA((5, CHUNKS)),
            pltpu.SemaphoreType.DMA((3, CHUNKS)), pltpu.SemaphoreType.DMA((3, CHUNKS)),
            pltpu.SemaphoreType.DMA((24,)), pltpu.SemaphoreType.DMA((8,)),
            pltpu.SemaphoreType.DMA((16,)),
        ],
        compiler_params=pltpu.CompilerParams(
            collective_id=1, has_side_effects=True, vmem_limit_bytes=VMEM_LIMIT
        ),
        name="far_and_gram",
    )(field_levels, bond_levels, previous, current)
    return tuple(
        pl.pallas_call(
            last_kernel,
            out_shape=(jax.ShapeDtypeStruct(block, f32), jax.ShapeDtypeStruct((32, 32), f32)),
            in_specs=[pl.BlockSpec(memory_space=pltpu.VMEM), hbm],
            out_specs=(hbm, hbm),
            scratch_shapes=[
                pltpu.VMEM(block, f32), pltpu.VMEM(block, f32), pltpu.VMEM((32, 32), f32),
                pltpu.SemaphoreType.DMA((TILES,)), pltpu.SemaphoreType.DMA((TILES,)),
                pltpu.SemaphoreType.DMA,
            ],
            compiler_params=pltpu.CompilerParams(vmem_limit_bytes=VMEM_LIMIT),
            name="factor_and_apply",
        )(gram, filtered)
    )


def solution(mesh):
    in_specs = (P(None, ("hi", "lo")), P(None, ("hi", "lo")), P(), P())
    out_specs = (P(None, ("hi", "lo")), P())
    return jax.shard_map(local, mesh=mesh, in_specs=in_specs, out_specs=out_specs, check_vma=False)
```

```python
import functools

import jax
import jax.numpy as jnp
from jax import lax
from jax.experimental import pallas as pl
from jax.experimental.pallas import tpu as pltpu
from jax.sharding import PartitionSpec as P

MESH = pl.DeviceIdType.MESH
HIGHEST = lax.Precision.HIGHEST
VECTORS = 32
AMPS = 16384
TOTAL = 2097152
SITES = 21
SCALE = 4.0 / SITES
CHUNKS = 16
HOP = 2
WIDTH = AMPS // CHUNKS
TOPS = WIDTH // 128
LAST_LAG = 3 * HOP
TILES = (8192, 6144, 2048)
VMEM_LIMIT = 66000000


def far_kernel(
    field_hbm, bond_hbm, previous_hbm, current_hbm, filtered_hbm, gram_ref,
    field_ref, bond_ref, current, previous, filtered, weights, direct, ring_z, ring_x, gram, first, second,
    load_sem, send_sem, relay_sem, direct_sem, z_sem, x_sem, small_send, first_sem, second_sem,
):
    hi = lax.axis_index("hi")
    lo = lax.axis_index("lo")
    core = lo & 1
    z = lo >> 1
    x = hi & 3
    y = hi >> 2
    z0, z1, x0, x1, y0, y1 = z & 1, z >> 1, x & 1, x >> 1, y & 1, y >> 1

    load_current = pltpu.make_async_copy(current_hbm, current, load_sem.at[0])
    load_previous = pltpu.make_async_copy(previous_hbm, previous, load_sem.at[1])
    load_field = pltpu.make_async_copy(field_hbm, field_ref, load_sem.at[2])
    load_bond = pltpu.make_async_copy(bond_hbm, bond_ref, load_sem.at[3])
    load_field.start()
    load_bond.start()
    load_current.start()
    load_previous.start()

    barrier = pltpu.get_barrier_semaphore()
    for i in range(1, 8):
        pl.semaphore_signal(barrier, inc=1, device_id=(hi, lo ^ i), device_id_type=MESH)
    for i in range(1, 16):
        pl.semaphore_signal(barrier, inc=1, device_id=(hi ^ i, lo), device_id_type=MESH)

    def columns(k):
        return pl.ds(pl.multiple_of(k * WIDTH, WIDTH), WIDTH)

    partners = [(hi, lo ^ 1), (hi, lo ^ 3), (hi, lo ^ 6), (hi ^ 3, lo), (hi ^ 12, lo)]
    takes = [None, core != z0, z0 != z1, x0 != x1, y0 != y1]

    def when(condition, body):
        if condition is None:
            body()
        else:
            pl.when(condition)(body)

    def direct_copy(i, cols, sem):
        return pltpu.make_async_remote_copy(
            src_ref=current.at[:, cols], dst_ref=direct.at[i, :, cols],
            send_sem=send_sem.at[i], recv_sem=sem, device_id=partners[i], device_id_type=MESH,
        )

    first_path = core == 0

    def ring_plan(spot, pair_bit, ring_device, pair_device):
        role = jnp.where(pair_bit == 1, spot, 3 - spot)

        def at_role(r):
            return ring_device(jnp.where(pair_bit == 1, r, 3 - r))

        def pick(condition, a, b):
            return tuple(jnp.where(condition, u, v) for u, v in zip(a, b))

        own_device = pick(first_path, at_role(jnp.where(role == 0, 3, 0)), pair_device)
        last_a = jnp.where(first_path, 2, 0)
        last_b = jnp.where(first_path, 0, 2)
        has_a = (role == 3) | (role == last_a)
        has_b = (role == 3) | (role == last_b)
        a_device = pick(
            first_path,
            pick(role == 3, at_role(2), pair_device),
            pick(role == 3, at_role(0), at_role(1)),
        )
        b_device = pick(
            first_path,
            pick(role == 3, pair_device, at_role(3)),
            pick(role == 3, at_role(0), at_role(3)),
        )
        return dict(
            active=role < 2, own=(own_device, jnp.where(role == 0, 0, 1)),
            relays=[
                (has_a, a_device, jnp.where(role == 3, 0, 2), jnp.where(role == 3, HOP, 2 * HOP)),
                (has_b, b_device, jnp.where(role == 3, 2, 1), jnp.where(role == 3, 2 * HOP, HOP)),
            ],
        )

    plans = [
        (ring_z, z_sem, 5, 0, ring_plan(z, x0, lambda s: (hi, s * 2 + core), (hi ^ 1, lo))),
        (ring_x, x_sem, 6, 2, ring_plan(x, y0, lambda s: (y * 4 + s, lo), (hi ^ 4, lo))),
    ]

    def own_copy(ring, k_cols, sem_index, plan, recv):
        device, slot = plan["own"]
        return pltpu.make_async_remote_copy(
            src_ref=current.at[:, k_cols], dst_ref=ring.at[slot, :, k_cols],
            send_sem=send_sem.at[sem_index], recv_sem=recv, device_id=device, device_id_type=MESH,
        )

    def relay_copy(ring, which, k_cols, sem_index, relay, recv):
        _, device, slot, _ = relay
        return pltpu.make_async_remote_copy(
            src_ref=ring.at[which, :, k_cols], dst_ref=ring.at[slot, :, k_cols],
            send_sem=relay_sem.at[sem_index], recv_sem=recv, device_id=device, device_id_type=MESH,
        )

    def arrived(ring, slot, sems, k):
        cols = columns(k)
        pltpu.make_async_remote_copy(
            src_ref=ring.at[slot, :, cols], dst_ref=ring.at[slot, :, cols],
            send_sem=relay_sem.at[0], recv_sem=sems.at[slot, k],
            device_id=(hi, lo ^ 1), device_id_type=MESH,
        ).wait_recv()

    def send_own(k):
        cols = columns(k)
        for i in (1, 2, 3, 4, 0):
            when(takes[i], lambda i=i: direct_copy(i, cols, direct_sem.at[i, k]).start())

    def send_ring(s):
        for ring, sems, index, _, plan in plans:
            slot = plan["own"][1]
            k = s

            @pl.when(plan["active"] & (k < CHUNKS))
            def _(ring=ring, sems=sems, index=index, plan=plan, slot=slot, k=k):
                own_copy(ring, columns(k), index, plan, sems.at[slot, k]).start()

    load_field.wait()
    load_bond.wait()
    level = [bond_ref[s].astype(jnp.float32) for s in range(SITES - 1)]
    field = [0.75 * field_ref[s].astype(jnp.float32) for s in range(SITES)]
    half = [0.25 * v for v in level]
    full = [0.5 * v for v in level]

    def spin(bit):
        return 0.5 - bit.astype(jnp.float32)

    rows = lax.broadcasted_iota(jnp.int32, (128, 128), 0)
    lanes = lax.broadcasted_iota(jnp.int32, (128, 128), 1)
    flips = jnp.zeros((128, 128), jnp.float32)
    for s in range(7, 13):
        b = s - 7
        hit = (((lanes >> b) ^ (lanes >> (b + 1))) & 1 == 1) & (rows == lanes ^ (3 << b))
        flips = flips + jnp.where(hit, half[s], 0.0)
    lane_diagonal = jnp.zeros((128, 128), jnp.float32)
    for s in range(7, 14):
        lane_diagonal = lane_diagonal + field[s] * spin(lanes >> (s - 7) & 1)
        if s < 13:
            lane_diagonal = lane_diagonal + full[s] * spin(lanes >> (s - 7) & 1) * spin(
                lanes >> (s - 6) & 1
            )
    lane_diagonal = lane_diagonal + full[13] * spin(core) * spin(lanes >> 6 & 1)
    for top in range(2):
        seam = lane_diagonal + full[6] * (0.5 - top) * spin(lanes & 1)
        weights[top, 0:128, :] = flips + jnp.where(rows == lanes, seam, 0.0)
        hit = (rows == lanes ^ 1) & (lanes & 1 != top)
        weights[top, 128:256, :] = jnp.where(hit, half[6], 0.0)
    bits = [core, z0, z1, x0, x1, y0, y1]
    device_part = field[20] * spin(y1)
    for i in range(6):
        device_part = device_part + field[14 + i] * spin(bits[i])
        device_part = device_part + full[14 + i] * spin(bits[i]) * spin(bits[i + 1])

    lane = lax.broadcasted_iota(jnp.int32, (VECTORS, WIDTH), 1)
    core_factor = jnp.where((lane >> 6 & 1) != core, SCALE * half[13], 0.0)
    gram[...] = jnp.zeros_like(gram)

    def top_columns(t):
        return pl.ds(pl.multiple_of(t * 128, 128), 128)

    def local_part(k):
        sums = []
        left = []
        for i in range(TOPS):
            t = k * TOPS + i
            spins = [spin(t >> s & 1) for s in range(7)]
            diagonal = device_part + field[6] * spins[6]
            for s in range(6):
                diagonal = diagonal + field[s] * spins[s] + full[s] * spins[s] * spins[s + 1]
            own = current[:, top_columns(t)]
            total = diagonal * own
            for s in range(6):
                differ = ((t >> s) ^ (t >> (s + 1)) & 1) & 1
                factor = half[s] * differ.astype(jnp.float32)
                total = total + factor * current[:, top_columns(t ^ (3 << s))]
            sums.append(total)
            left.append(jnp.concatenate([own, current[:, top_columns(t ^ 64)]], axis=1))
        product = jnp.dot(
            jnp.concatenate(left, axis=0), weights[k // (CHUNKS // 2)],
            precision=HIGHEST, preferred_element_type=jnp.float32,
        )
        for i in range(TOPS):
            where = top_columns(k * TOPS + i)
            filtered[:, where] = (
                SCALE * (sums[i] + product[i * VECTORS:(i + 1) * VECTORS]) - previous[:, where]
            )

    def consume(k):
        cols = columns(k)

        direct_copy(0, cols, direct_sem.at[0, k]).wait_recv()
        filtered[:, cols] += core_factor * jnp.concatenate(
            [
                pltpu.roll(direct[0, :, top_columns(k * TOPS + i)], 64, 1)
                for i in range(TOPS)
            ],
            axis=1,
        )
        for i, bond in ((1, 14), (2, 15), (3, 17), (4, 19)):
            def add(i=i, bond=bond):
                direct_copy(i, cols, direct_sem.at[i, k]).wait_recv()
                filtered[:, cols] += SCALE * half[bond] * direct[i, :, cols]
            when(takes[i], add)
        for (ring, sems, _, _, plan), bond in zip(plans, (16, 18)):
            def add(ring=ring, sems=sems, bond=bond):
                arrived(ring, 2, sems, k)
                filtered[:, cols] += SCALE * half[bond] * ring[2, :, cols]
            when(plan["active"], add)
        part = filtered[:, cols]
        gram[...] += lax.dot_general(
            part, part, (((1,), (1,)), ((), ())), precision=HIGHEST,
            preferred_element_type=jnp.float32,
        )

    load_current.wait()
    pl.semaphore_wait(barrier, 22)

    @pl.loop(0, CHUNKS + LAST_LAG)
    def _(s):
        send_ring(s)

        @pl.when(s < CHUNKS)
        def _():
            send_own(s)

        for ring, sems, _, base, plan in plans:
            for which in range(2):
                relay = plan["relays"][which]
                has, _, slot, lag = relay
                k = s - lag

                @pl.when(has & (k >= 0) & (k < CHUNKS))
                def _(ring=ring, sems=sems, base=base, which=which, relay=relay, slot=slot, k=k):
                    arrived(ring, which, sems, k)
                    relay_copy(
                        ring, which, columns(k), base + which, relay, sems.at[slot, k]
                    ).start()

        @pl.when(s < CHUNKS)
        def _():
            @pl.when(s == 0)
            def _():
                load_previous.wait()

            local_part(s)

        @pl.when(s >= LAST_LAG)
        def _():
            consume(s - LAST_LAG)

    store = pltpu.make_async_copy(filtered, filtered_hbm, load_sem.at[0])
    store.start()

    g = gram[...]
    packed = jnp.concatenate([g[8 * i:8 * i + 8, :] for i in range(4)], axis=1)
    for size, spot, box, sems, base, device in (
        (8, lo, first, first_sem, 0, lambda i: (hi, lo ^ i)),
        (16, hi, second, second_sem, 8, lambda i: (hi ^ i, lo)),
    ):
        box[spot] = packed

        def small(i):
            return pltpu.make_async_remote_copy(
                src_ref=box.at[spot], dst_ref=box.at[spot], send_sem=small_send.at[base + i],
                recv_sem=sems.at[spot], device_id=device(i), device_id_type=MESH,
            )

        for i in range(1, size):
            small(i).start()
        for i in range(1, size):
            other = spot ^ i
            pltpu.make_async_remote_copy(
                src_ref=box.at[other], dst_ref=box.at[other], send_sem=small_send.at[base + i],
                recv_sem=sems.at[other], device_id=device(i), device_id_type=MESH,
            ).wait_recv()
        packed = box[0]
        for i in range(1, size):
            packed = packed + box[i]
    gram_ref[...] = packed * (1.0 / TOTAL)

    whole = pl.ds(0, AMPS)
    for i in range(5):
        when(takes[i], lambda i=i: direct_copy(i, whole, direct_sem.at[i, 0]).wait_send())
    for ring, sems, index, base, plan in plans:
        when(plan["active"], lambda ring=ring, sems=sems, index=index, plan=plan:
             own_copy(ring, whole, index, plan, sems.at[0, 0]).wait_send())
        for which in range(2):
            relay = plan["relays"][which]
            when(relay[0], lambda ring=ring, sems=sems, base=base, which=which, relay=relay:
                 relay_copy(ring, which, whole, base + which, relay, sems.at[0, 0]).wait_send())
    for size, spot, box, sems, base, device in (
        (8, lo, first, first_sem, 0, lambda i: (hi, lo ^ i)),
        (16, hi, second, second_sem, 8, lambda i: (hi ^ i, lo)),
    ):
        for i in range(1, size):
            pltpu.make_async_remote_copy(
                src_ref=box.at[spot], dst_ref=box.at[spot], send_sem=small_send.at[base + i],
                recv_sem=sems.at[spot], device_id=device(i), device_id_type=MESH,
            ).wait_send()
    store.wait()


def last_kernel(
    gram_ref, filtered_hbm, ortho_hbm, upper_hbm, filtered, ortho, upper, load_sem, store_sem, upper_sem
):
    edges = [sum(TILES[:i]) for i in range(len(TILES))]

    def load(i):
        cols = pl.ds(edges[i], TILES[i])
        return pltpu.make_async_copy(filtered_hbm.at[:, cols], filtered.at[:, cols], load_sem.at[i])

    def store(i):
        cols = pl.ds(edges[i], TILES[i])
        return pltpu.make_async_copy(ortho.at[:, cols], ortho_hbm.at[:, cols], store_sem.at[i])

    for i in range(len(TILES)):
        load(i).start()

    packed = gram_ref[...]
    parts = [packed] + [pltpu.roll(packed, 128 - 32 * i, 1) for i in range(1, 4)]
    table = jnp.concatenate(parts, axis=0)
    row = lax.broadcasted_iota(jnp.int32, (VECTORS, 128), 0)
    lane = lax.broadcasted_iota(jnp.int32, (VECTORS, 128), 1)
    table = jnp.where(lane < 32, table, jnp.where(lane - 32 == row, 1.0, 0.0))
    for j in range(VECTORS - 1):
        factor = table[:, j:j + 1] / table[j:j + 1, j:j + 1]
        factor = jnp.where(row[:, 0:1] > j, factor, 0.0)
        table = table - factor * table[j:j + 1, :]
    pivots = jnp.sum(jnp.where(row == lane, table, 0.0), axis=1, keepdims=True)
    table = table / jnp.sqrt(pivots)
    upper[...] = jnp.where(lane >= row, table, 0.0)[:, 0:32]
    store_upper = pltpu.make_async_copy(upper, upper_hbm, upper_sem)
    store_upper.start()
    inverse = pltpu.roll(table, 96, 1)[:, 0:32]

    def split(values):
        high = values.astype(jnp.bfloat16)
        rest = values - high.astype(jnp.float32)
        middle = rest.astype(jnp.bfloat16)
        low = (rest - middle.astype(jnp.float32)).astype(jnp.bfloat16)
        return high, middle, low

    high, middle, low = split(inverse)
    none = jnp.zeros_like(high)
    left = jnp.concatenate(
        [
            jnp.concatenate([high, high, high], axis=1),
            jnp.concatenate([middle, middle, none], axis=1),
            jnp.concatenate([low, none, none], axis=1),
        ],
        axis=0,
    )
    for i in range(len(TILES)):
        load(i).wait()
        cols = pl.ds(edges[i], TILES[i])
        right = jnp.concatenate(split(filtered[:, cols]), axis=0)
        parts = jnp.dot(left, right, preferred_element_type=jnp.float32)
        ortho[:, cols] = parts[0:32] + (parts[32:64] + parts[64:96])
        store(i).start()
    for i in range(len(TILES)):
        store(i).wait()
    store_upper.wait()


def local(previous, current, field_levels, bond_levels):
    hbm = pl.BlockSpec(memory_space=pltpu.HBM)
    block = (VECTORS, AMPS)
    f32 = jnp.float32
    filtered, gram = pl.pallas_call(
        far_kernel,
        out_shape=(jax.ShapeDtypeStruct(block, f32), jax.ShapeDtypeStruct((8, 128), f32)),
        in_specs=[
            hbm, hbm, hbm, hbm,
        ],
        out_specs=(hbm, pl.BlockSpec(memory_space=pltpu.VMEM)),
        scratch_shapes=[
            pltpu.SMEM((SITES,), jnp.int32), pltpu.SMEM((SITES - 1,), jnp.int32),
            pltpu.VMEM(block, f32), pltpu.VMEM(block, f32), pltpu.VMEM(block, f32),
            pltpu.VMEM((2, 256, 128), f32),
            pltpu.VMEM((5,) + block, f32), pltpu.VMEM((3,) + block, f32),
            pltpu.VMEM((3,) + block, f32),
            pltpu.VMEM((VECTORS, VECTORS), f32),
            pltpu.VMEM((8, 8, 128), f32), pltpu.VMEM((16, 8, 128), f32),
            pltpu.SemaphoreType.DMA((4,)), pltpu.SemaphoreType.DMA((7,)),
            pltpu.SemaphoreType.DMA((4,)), pltpu.SemaphoreType.DMA((5, CHUNKS)),
            pltpu.SemaphoreType.DMA((3, CHUNKS)), pltpu.SemaphoreType.DMA((3, CHUNKS)),
            pltpu.SemaphoreType.DMA((24,)), pltpu.SemaphoreType.DMA((8,)),
            pltpu.SemaphoreType.DMA((16,)),
        ],
        compiler_params=pltpu.CompilerParams(
            collective_id=1, has_side_effects=True, vmem_limit_bytes=VMEM_LIMIT
        ),
        name="far_and_gram",
    )(field_levels, bond_levels, previous, current)
    return tuple(
        pl.pallas_call(
            last_kernel,
            out_shape=(jax.ShapeDtypeStruct(block, f32), jax.ShapeDtypeStruct((32, 32), f32)),
            in_specs=[pl.BlockSpec(memory_space=pltpu.VMEM), hbm],
            out_specs=(hbm, hbm),
            scratch_shapes=[
                pltpu.VMEM(block, f32), pltpu.VMEM(block, f32), pltpu.VMEM((32, 32), f32),
                pltpu.SemaphoreType.DMA((len(TILES),)), pltpu.SemaphoreType.DMA((len(TILES),)),
                pltpu.SemaphoreType.DMA,
            ],
            compiler_params=pltpu.CompilerParams(vmem_limit_bytes=VMEM_LIMIT),
            name="factor_and_apply",
        )(gram, filtered)
    )


def solution(mesh):
    in_specs = (P(None, ("hi", "lo")), P(None, ("hi", "lo")), P(), P())
    out_specs = (P(None, ("hi", "lo")), P())
    return jax.shard_map(local, mesh=mesh, in_specs=in_specs, out_specs=out_specs, check_vma=False)
```

```python
import functools

import jax
import jax.numpy as jnp
from jax import lax
from jax.experimental import pallas as pl
from jax.experimental.pallas import tpu as pltpu
from jax.sharding import PartitionSpec as P

MESH = pl.DeviceIdType.MESH
HIGHEST = lax.Precision.HIGHEST
VECTORS = 32
AMPS = 16384
TOTAL = 2097152
SITES = 21
SCALE = 4.0 / SITES
CHUNKS = 16
HOP = 2
WIDTH = AMPS // CHUNKS
TOPS = WIDTH // 128
LAST_LAG = 3 * HOP
TILES = (8192, 6144, 2048)
VMEM_LIMIT = 66000000


def far_kernel(
    field_hbm, bond_hbm, previous_hbm, current_hbm, filtered_hbm, gram_ref,
    field_ref, bond_ref, current, previous, filtered, weights, direct, ring_z, ring_x, gram, first, second,
    load_sem, send_sem, relay_sem, direct_sem, z_sem, x_sem, small_send, first_sem, second_sem,
):
    hi = lax.axis_index("hi")
    lo = lax.axis_index("lo")
    core = lo & 1
    z = lo >> 1
    x = hi & 3
    y = hi >> 2
    z0, z1, x0, x1, y0, y1 = z & 1, z >> 1, x & 1, x >> 1, y & 1, y >> 1

    load_current = pltpu.make_async_copy(current_hbm, current, load_sem.at[0])
    load_previous = pltpu.make_async_copy(previous_hbm, previous, load_sem.at[1])
    load_field = pltpu.make_async_copy(field_hbm, field_ref, load_sem.at[2])
    load_bond = pltpu.make_async_copy(bond_hbm, bond_ref, load_sem.at[3])
    load_field.start()
    load_bond.start()
    load_current.start()
    load_previous.start()

    barrier = pltpu.get_barrier_semaphore()
    for i in range(1, 8):
        pl.semaphore_signal(barrier, inc=1, device_id=(hi, lo ^ i), device_id_type=MESH)
    for i in range(1, 16):
        pl.semaphore_signal(barrier, inc=1, device_id=(hi ^ i, lo), device_id_type=MESH)

    def columns(k):
        return pl.ds(pl.multiple_of(k * WIDTH, WIDTH), WIDTH)

    partners = [(hi, lo ^ 1), (hi, lo ^ 3), (hi, lo ^ 6), (hi ^ 3, lo), (hi ^ 12, lo)]
    takes = [None, core != z0, z0 != z1, x0 != x1, y0 != y1]

    def when(condition, body):
        if condition is None:
            body()
        else:
            pl.when(condition)(body)

    def direct_copy(i, cols, sem):
        return pltpu.make_async_remote_copy(
            src_ref=current.at[:, cols], dst_ref=direct.at[i, :, cols],
            send_sem=send_sem.at[i], recv_sem=sem, device_id=partners[i], device_id_type=MESH,
        )

    first_path = core == 0

    def ring_plan(spot, pair_bit, ring_device, pair_device):
        role = jnp.where(pair_bit == 1, spot, 3 - spot)

        def at_role(r):
            return ring_device(jnp.where(pair_bit == 1, r, 3 - r))

        def pick(condition, a, b):
            return tuple(jnp.where(condition, u, v) for u, v in zip(a, b))

        own_device = pick(first_path, at_role(jnp.where(role == 0, 3, 0)), pair_device)
        last_a = jnp.where(first_path, 2, 0)
        last_b = jnp.where(first_path, 0, 2)
        has_a = (role == 3) | (role == last_a)
        has_b = (role == 3) | (role == last_b)
        a_device = pick(
            first_path,
            pick(role == 3, at_role(2), pair_device),
            pick(role == 3, at_role(0), at_role(1)),
        )
        b_device = pick(
            first_path,
            pick(role == 3, pair_device, at_role(3)),
            pick(role == 3, at_role(0), at_role(3)),
        )
        return dict(
            active=role < 2, own=(own_device, jnp.where(role == 0, 0, 1)),
            relays=[
                (has_a, a_device, jnp.where(role == 3, 0, 2), jnp.where(role == 3, HOP, 2 * HOP)),
                (has_b, b_device, jnp.where(role == 3, 2, 1), jnp.where(role == 3, 2 * HOP, HOP)),
            ],
        )

    plans = [
        (ring_z, z_sem, 5, 0, ring_plan(z, x0, lambda s: (hi, s * 2 + core), (hi ^ 1, lo))),
        (ring_x, x_sem, 6, 2, ring_plan(x, y0, lambda s: (y * 4 + s, lo), (hi ^ 4, lo))),
    ]

    def own_copy(ring, k_cols, sem_index, plan, recv):
        device, slot = plan["own"]
        return pltpu.make_async_remote_copy(
            src_ref=current.at[:, k_cols], dst_ref=ring.at[slot, :, k_cols],
            send_sem=send_sem.at[sem_index], recv_sem=recv, device_id=device, device_id_type=MESH,
        )

    def relay_copy(ring, which, k_cols, sem_index, relay, recv):
        _, device, slot, _ = relay
        return pltpu.make_async_remote_copy(
            src_ref=ring.at[which, :, k_cols], dst_ref=ring.at[slot, :, k_cols],
            send_sem=relay_sem.at[sem_index], recv_sem=recv, device_id=device, device_id_type=MESH,
        )

    def arrived(ring, slot, sems, k):
        cols = columns(k)
        pltpu.make_async_remote_copy(
            src_ref=ring.at[slot, :, cols], dst_ref=ring.at[slot, :, cols],
            send_sem=relay_sem.at[0], recv_sem=sems.at[slot, k],
            device_id=(hi, lo ^ 1), device_id_type=MESH,
        ).wait_recv()

    def send_own(k):
        cols = columns(k)
        for i in (1, 2, 3, 4, 0):
            when(takes[i], lambda i=i: direct_copy(i, cols, direct_sem.at[i, k]).start())

    def send_ring(s):
        for ring, sems, index, _, plan in plans:
            slot = plan["own"][1]
            k = s

            @pl.when(plan["active"] & (k < CHUNKS))
            def _(ring=ring, sems=sems, index=index, plan=plan, slot=slot, k=k):
                own_copy(ring, columns(k), index, plan, sems.at[slot, k]).start()

    load_field.wait()
    load_bond.wait()
    level = [bond_ref[s].astype(jnp.float32) for s in range(SITES - 1)]
    field = [0.75 * field_ref[s].astype(jnp.float32) for s in range(SITES)]
    half = [0.25 * v for v in level]
    full = [0.5 * v for v in level]

    def spin(bit):
        return 0.5 - bit.astype(jnp.float32)

    rows = lax.broadcasted_iota(jnp.int32, (128, 128), 0)
    lanes = lax.broadcasted_iota(jnp.int32, (128, 128), 1)
    flips = jnp.zeros((128, 128), jnp.float32)
    for s in range(7, 13):
        b = s - 7
        hit = (((lanes >> b) ^ (lanes >> (b + 1))) & 1 == 1) & (rows == lanes ^ (3 << b))
        flips = flips + jnp.where(hit, half[s], 0.0)
    lane_diagonal = jnp.zeros((128, 128), jnp.float32)
    for s in range(7, 14):
        lane_diagonal = lane_diagonal + field[s] * spin(lanes >> (s - 7) & 1)
        if s < 13:
            lane_diagonal = lane_diagonal + full[s] * spin(lanes >> (s - 7) & 1) * spin(
                lanes >> (s - 6) & 1
            )
    lane_diagonal = lane_diagonal + full[13] * spin(core) * spin(lanes >> 6 & 1)
    for top in range(2):
        seam = lane_diagonal + full[6] * (0.5 - top) * spin(lanes & 1)
        weights[top, 0:128, :] = flips + jnp.where(rows == lanes, seam, 0.0)
        hit = (rows == lanes ^ 1) & (lanes & 1 != top)
        weights[top, 128:256, :] = jnp.where(hit, half[6], 0.0)
    bits = [core, z0, z1, x0, x1, y0, y1]
    device_part = field[20] * spin(y1)
    for i in range(6):
        device_part = device_part + field[14 + i] * spin(bits[i])
        device_part = device_part + full[14 + i] * spin(bits[i]) * spin(bits[i + 1])

    lane = lax.broadcasted_iota(jnp.int32, (VECTORS, WIDTH), 1)
    core_factor = jnp.where((lane >> 6 & 1) != core, SCALE * half[13], 0.0)
    gram[...] = jnp.zeros_like(gram)

    def top_columns(t):
        return pl.ds(pl.multiple_of(t * 128, 128), 128)

    def local_part(k):
        sums = []
        left = []
        for i in range(TOPS):
            t = k * TOPS + i
            spins = [spin(t >> s & 1) for s in range(7)]
            diagonal = device_part + field[6] * spins[6]
            for s in range(6):
                diagonal = diagonal + field[s] * spins[s] + full[s] * spins[s] * spins[s + 1]
            own = current[:, top_columns(t)]
            total = diagonal * own
            for s in range(6):
                differ = ((t >> s) ^ (t >> (s + 1)) & 1) & 1
                factor = half[s] * differ.astype(jnp.float32)
                total = total + factor * current[:, top_columns(t ^ (3 << s))]
            sums.append(total)
            left.append(jnp.concatenate([own, current[:, top_columns(t ^ 64)]], axis=1))
        product = jnp.dot(
            jnp.concatenate(left, axis=0), weights[k // (CHUNKS // 2)],
            precision=HIGHEST, preferred_element_type=jnp.float32,
        )
        for i in range(TOPS):
            where = top_columns(k * TOPS + i)
            filtered[:, where] = (
                SCALE * (sums[i] + product[i * VECTORS:(i + 1) * VECTORS]) - previous[:, where]
            )

    def consume(k):
        cols = columns(k)

        direct_copy(0, cols, direct_sem.at[0, k]).wait_recv()
        filtered[:, cols] += core_factor * jnp.concatenate(
            [
                pltpu.roll(direct[0, :, top_columns(k * TOPS + i)], 64, 1)
                for i in range(TOPS)
            ],
            axis=1,
        )
        for i, bond in ((1, 14), (2, 15), (3, 17), (4, 19)):
            def add(i=i, bond=bond):
                direct_copy(i, cols, direct_sem.at[i, k]).wait_recv()
                filtered[:, cols] += SCALE * half[bond] * direct[i, :, cols]
            when(takes[i], add)
        for (ring, sems, _, _, plan), bond in zip(plans, (16, 18)):
            def add(ring=ring, sems=sems, bond=bond):
                arrived(ring, 2, sems, k)
                filtered[:, cols] += SCALE * half[bond] * ring[2, :, cols]
            when(plan["active"], add)
        part = filtered[:, cols]
        gram[...] += lax.dot_general(
            part, part, (((1,), (1,)), ((), ())), precision=HIGHEST,
            preferred_element_type=jnp.float32,
        )

    load_current.wait()
    pl.semaphore_wait(barrier, 22)

    @pl.loop(0, CHUNKS + LAST_LAG)
    def _(s):
        send_ring(s)

        @pl.when(s < CHUNKS)
        def _():
            send_own(s)

        for ring, sems, _, base, plan in plans:
            for which in range(2):
                relay = plan["relays"][which]
                has, _, slot, lag = relay
                k = s - lag

                @pl.when(has & (k >= 0) & (k < CHUNKS))
                def _(ring=ring, sems=sems, base=base, which=which, relay=relay, slot=slot, k=k):
                    arrived(ring, which, sems, k)
                    relay_copy(
                        ring, which, columns(k), base + which, relay, sems.at[slot, k]
                    ).start()

        @pl.when(s < CHUNKS)
        def _():
            @pl.when(s == 0)
            def _():
                load_previous.wait()

            local_part(s)

        @pl.when(s >= LAST_LAG)
        def _():
            consume(s - LAST_LAG)

    store = pltpu.make_async_copy(filtered, filtered_hbm, load_sem.at[0])
    store.start()

    g = gram[...]
    packed = jnp.concatenate([g[8 * i:8 * i + 8, :] for i in range(4)], axis=1)
    for size, spot, box, sems, base, device in (
        (8, lo, first, first_sem, 0, lambda i: (hi, lo ^ i)),
        (16, hi, second, second_sem, 8, lambda i: (hi ^ i, lo)),
    ):
        box[spot] = packed

        def small(i):
            return pltpu.make_async_remote_copy(
                src_ref=box.at[spot], dst_ref=box.at[spot], send_sem=small_send.at[base + i],
                recv_sem=sems.at[spot], device_id=device(i), device_id_type=MESH,
            )

        for i in range(1, size):
            small(i).start()
        for i in range(1, size):
            other = spot ^ i
            pltpu.make_async_remote_copy(
                src_ref=box.at[other], dst_ref=box.at[other], send_sem=small_send.at[base + i],
                recv_sem=sems.at[other], device_id=device(i), device_id_type=MESH,
            ).wait_recv()
        packed = box[0]
        for i in range(1, size):
            packed = packed + box[i]
    gram_ref[...] = packed * (1.0 / TOTAL)

    whole = pl.ds(0, AMPS)
    for i in range(5):
        when(takes[i], lambda i=i: direct_copy(i, whole, direct_sem.at[i, 0]).wait_send())
    for ring, sems, index, base, plan in plans:
        when(plan["active"], lambda ring=ring, sems=sems, index=index, plan=plan:
             own_copy(ring, whole, index, plan, sems.at[0, 0]).wait_send())
        for which in range(2):
            relay = plan["relays"][which]
            when(relay[0], lambda ring=ring, sems=sems, base=base, which=which, relay=relay:
                 relay_copy(ring, which, whole, base + which, relay, sems.at[0, 0]).wait_send())
    for size, spot, box, sems, base, device in (
        (8, lo, first, first_sem, 0, lambda i: (hi, lo ^ i)),
        (16, hi, second, second_sem, 8, lambda i: (hi ^ i, lo)),
    ):
        for i in range(1, size):
            pltpu.make_async_remote_copy(
                src_ref=box.at[spot], dst_ref=box.at[spot], send_sem=small_send.at[base + i],
                recv_sem=sems.at[spot], device_id=device(i), device_id_type=MESH,
            ).wait_send()
    store.wait()


def last_kernel(
    gram_ref, filtered_hbm, ortho_hbm, upper_hbm, filtered, ortho, upper, load_sem, store_sem, upper_sem
):
    edges = [sum(TILES[:i]) for i in range(len(TILES))]

    def load(i):
        cols = pl.ds(edges[i], TILES[i])
        return pltpu.make_async_copy(filtered_hbm.at[:, cols], filtered.at[:, cols], load_sem.at[i])

    def store(i):
        cols = pl.ds(edges[i], TILES[i])
        return pltpu.make_async_copy(ortho.at[:, cols], ortho_hbm.at[:, cols], store_sem.at[i])

    for i in range(len(TILES)):
        load(i).start()

    packed = gram_ref[...]
    parts = [packed] + [pltpu.roll(packed, 128 - 32 * i, 1) for i in range(1, 4)]
    table = jnp.concatenate(parts, axis=0)
    row = lax.broadcasted_iota(jnp.int32, (VECTORS, 128), 0)
    lane = lax.broadcasted_iota(jnp.int32, (VECTORS, 128), 1)
    table = jnp.where(lane < 32, table, jnp.where(lane - 32 == row, 1.0, 0.0))
    for j in range(VECTORS - 1):
        factor = table[:, j:j + 1] / table[j:j + 1, j:j + 1]
        factor = jnp.where(row[:, 0:1] > j, factor, 0.0)
        table = table - factor * table[j:j + 1, :]
    pivots = jnp.sum(jnp.where(row == lane, table, 0.0), axis=1, keepdims=True)
    table = table / jnp.sqrt(pivots)
    upper[...] = jnp.where(lane >= row, table, 0.0)[:, 0:32]
    store_upper = pltpu.make_async_copy(upper, upper_hbm, upper_sem)
    store_upper.start()
    inverse = pltpu.roll(table, 96, 1)[:, 0:32]

    def split(values):
        high = values.astype(jnp.bfloat16)
        rest = values - high.astype(jnp.float32)
        middle = rest.astype(jnp.bfloat16)
        return high, middle

    high, middle = split(inverse)
    none = jnp.zeros_like(high)
    left = jnp.concatenate(
        [jnp.concatenate([high, high], axis=1), jnp.concatenate([middle, none], axis=1)], axis=0
    )
    for i in range(len(TILES)):
        load(i).wait()
        cols = pl.ds(edges[i], TILES[i])
        right = jnp.concatenate(split(filtered[:, cols]), axis=0)
        parts = jnp.dot(left, right, preferred_element_type=jnp.float32)
        ortho[:, cols] = parts[0:32] + parts[32:64]
        store(i).start()
    for i in range(len(TILES)):
        store(i).wait()
    store_upper.wait()


def local(previous, current, field_levels, bond_levels):
    hbm = pl.BlockSpec(memory_space=pltpu.HBM)
    block = (VECTORS, AMPS)
    f32 = jnp.float32
    filtered, gram = pl.pallas_call(
        far_kernel,
        out_shape=(jax.ShapeDtypeStruct(block, f32), jax.ShapeDtypeStruct((8, 128), f32)),
        in_specs=[
            hbm, hbm, hbm, hbm,
        ],
        out_specs=(hbm, pl.BlockSpec(memory_space=pltpu.VMEM)),
        scratch_shapes=[
            pltpu.SMEM((SITES,), jnp.int32), pltpu.SMEM((SITES - 1,), jnp.int32),
            pltpu.VMEM(block, f32), pltpu.VMEM(block, f32), pltpu.VMEM(block, f32),
            pltpu.VMEM((2, 256, 128), f32),
            pltpu.VMEM((5,) + block, f32), pltpu.VMEM((3,) + block, f32),
            pltpu.VMEM((3,) + block, f32),
            pltpu.VMEM((VECTORS, VECTORS), f32),
            pltpu.VMEM((8, 8, 128), f32), pltpu.VMEM((16, 8, 128), f32),
            pltpu.SemaphoreType.DMA((4,)), pltpu.SemaphoreType.DMA((7,)),
            pltpu.SemaphoreType.DMA((4,)), pltpu.SemaphoreType.DMA((5, CHUNKS)),
            pltpu.SemaphoreType.DMA((3, CHUNKS)), pltpu.SemaphoreType.DMA((3, CHUNKS)),
            pltpu.SemaphoreType.DMA((24,)), pltpu.SemaphoreType.DMA((8,)),
            pltpu.SemaphoreType.DMA((16,)),
        ],
        compiler_params=pltpu.CompilerParams(
            collective_id=1, has_side_effects=True, vmem_limit_bytes=VMEM_LIMIT
        ),
        name="far_and_gram",
    )(field_levels, bond_levels, previous, current)
    return tuple(
        pl.pallas_call(
            last_kernel,
            out_shape=(jax.ShapeDtypeStruct(block, f32), jax.ShapeDtypeStruct((32, 32), f32)),
            in_specs=[pl.BlockSpec(memory_space=pltpu.VMEM), hbm],
            out_specs=(hbm, hbm),
            scratch_shapes=[
                pltpu.VMEM(block, f32), pltpu.VMEM(block, f32), pltpu.VMEM((32, 32), f32),
                pltpu.SemaphoreType.DMA((len(TILES),)), pltpu.SemaphoreType.DMA((len(TILES),)),
                pltpu.SemaphoreType.DMA,
            ],
            compiler_params=pltpu.CompilerParams(vmem_limit_bytes=VMEM_LIMIT),
            name="factor_and_apply",
        )(gram, filtered)
    )


def solution(mesh):
    in_specs = (P(None, ("hi", "lo")), P(None, ("hi", "lo")), P(), P())
    out_specs = (P(None, ("hi", "lo")), P())
    return jax.shard_map(local, mesh=mesh, in_specs=in_specs, out_specs=out_specs, check_vma=False)
```
